512 devices in a mesh: slab: 64 (over z, y), mode: 8 (over x, core).
Axes of the slice: x: 4, y: 8, z: 8, core: 2. Of those that a mesh axis runs over, the one named last changes fastest.
Arguments:
- block_input: float32 [64, 512, 2048], P('mode', 'slab'), may hold values from -6 to 6
- drum_mask: int32 [512, 2048], P('slab'), may hold values 0 or 1
- panel: float32 [64, 512, 2048], P('mode', 'slab'), may hold values from -120 to 120, as said below
Outputs:
- filtered: float32 [64, 512, 2048], P('mode', 'slab')
- orthonormal: float32 [64, 512, 2048], P('mode', 'slab')
The draws below stay inside these ranges and needn't reach their ends.
Inputs may be any that keep to these rules, and one draw needn't show every extreme that they name: The panel's entries.
All inputs are finite; a program needn't handle non-finite values. No bound on the sum of `drum_mask` on one device may be relied on, other than what follows from the above.
Results may differ from the reference program's by a relative error of at most 0.000096.
Values sent between devices are 32-bit elements; how exact they have to be, the bound alone decides.
A program may use at most 64 MiB of HBM per device.

```python
import math
import jax
import jax.numpy as jnp
from jax import lax

BLOCK = 64
COLS = 2048
DEGREE = 8
NROWS = 512


def draw_panel(key, part):
    key_base, key_cell, key_column = jax.random.split(jax.random.fold_in(key, 11), 3)
    shape = (BLOCK, NROWS, COLS)
    base = jax.random.truncated_normal(key_base, -4.0, 4.0, shape, jnp.float32)
    cell_scale = jnp.exp(jax.random.uniform(key_cell, (NROWS, COLS), jnp.float32) * math.log(10.0))
    trend = jnp.exp(math.log(3.0) * jnp.arange(NROWS, dtype=jnp.float32) / NROWS)[:, None]
    column_scale = jnp.exp(jax.random.uniform(key_column, (BLOCK, 1, 1), jnp.float32) * math.log(10.0))
    return (base * cell_scale * trend * column_scale / 10.0).astype(jnp.float32)


def set_ends(drawn, own_key, low, high):
    extent = drawn.shape
    spot = [jax.random.randint(jax.random.fold_in(own_key, axis), (), 0, extent[axis]) for axis in range(len(extent))]
    drawn = drawn.at[tuple(spot)].set(low)
    longest = extent.index(max(extent))
    spot[longest] = (spot[longest] + 1) % extent[longest]
    return drawn.at[tuple(spot)].set(high)


def shard_levels(stream_key, extent, pieces, smallest, largest):
    def one(axis_at, blocks):
        steps = jax.random.uniform(jax.random.fold_in(jax.random.fold_in(stream_key, 6), axis_at), (blocks,), jnp.float32, smallest / len(pieces), largest / len(pieces))
        return jnp.repeat(jnp.exp(steps), extent[axis_at] // blocks).reshape((-1,) + (1,) * (len(extent) - axis_at - 1))

    loudness = one(*pieces[0])
    for cut in pieces[1:]:
        loudness = loudness * one(*cut)
    return loudness


def noise(key, extent, deviation, bound, pieces=(), kind=jnp.bfloat16):
    entries = deviation * jax.random.normal(key, extent, jnp.float32)
    if pieces:
        entries = entries * shard_levels(key, extent, pieces, -0.22, 0.18)
    return jnp.clip(entries, -bound, bound).astype(kind)


def setup_inputs(seed: int = 0) -> dict:
    splits = jax.random.split(jax.random.key(seed), 4)
    return {
        "block_input": noise(splits[0], (BLOCK, NROWS, COLS), 1.0, 6.0, ((0, 8), (1, 64)), jnp.float32),
        "drum_mask": set_ends((jax.random.randint(splits[1], (NROWS, COLS), 0, 4) < 3).astype(jnp.int32), jax.random.fold_in(splits[1], 1), 0, 1),
        "panel": draw_panel(jax.random.fold_in(splits[3], 71), 0),
    }


center_point = 5.0
half_width = 3.0
floor_estimate = 0.0

def filter_coefficients():
    sigma_first = half_width / (floor_estimate - center_point)
    result = [(sigma_first / half_width, 0.0)]
    sigma_now = sigma_first
    for step in range(DEGREE - 1):
        sigma_next = 1.0 / (2.0 / sigma_first - sigma_now)
        result.append((2.0 * sigma_next / half_width, sigma_now * sigma_next))
        sigma_now = sigma_next
    return result

def operate(field, mask_float):
    padded = jnp.pad(field, ((0, 0), (1, 1), (1, 1)))
    beside = padded[:, 2:, 1:-1] + padded[:, :-2, 1:-1] + padded[:, 1:-1, 2:] + padded[:, 1:-1, :-2]
    return mask_float * (4.0 * field - beside)

def chol_solve(factor, rhs):
    inner = lax.linalg.triangular_solve(factor, rhs, left_side=True, lower=True)
    return lax.linalg.triangular_solve(factor, inner, left_side=True, lower=True, transpose_a=True)

def reference(block_input, drum_mask, panel):
    highest = lax.Precision.HIGHEST
    mask_float = drum_mask.astype(jnp.float32)
    current = block_input * mask_float
    previous = current
    for scale_img, scale_old in filter_coefficients():
        applied = operate(current, mask_float)
        newest = scale_img * (applied - center_point * current)
        if scale_old != 0.0:
            newest = newest - scale_old * previous
        previous, current = (current, newest)
    filtered = current
    filtered_mat = filtered.reshape(BLOCK, -1)
    panel_mat = panel.reshape(BLOCK, -1)
    gram_zz = jnp.dot(filtered_mat, filtered_mat.T, precision=highest)
    cross_gram = jnp.dot(filtered_mat, panel_mat.T, precision=highest)
    factor_zz = jnp.linalg.cholesky(gram_zz)
    project = chol_solve(factor_zz, cross_gram)
    panel_new = panel_mat - jnp.dot(project.T, filtered_mat, precision=highest)
    gram_new = jnp.dot(panel_new, panel_new.T, precision=highest) / (NROWS * COLS)
    lower_part = jnp.linalg.cholesky(gram_new)
    orthonormal = lax.linalg.triangular_solve(lower_part, panel_new, left_side=True, lower=True)
    return (filtered, orthonormal.reshape(panel.shape))
```

```python
import functools

import jax
import jax.numpy as jnp
from jax import lax
from jax.experimental import pallas as pl
from jax.experimental.pallas import tpu as pltpu
from jax.sharding import PartitionSpec as P

DEGREE = 8
ROWS_Y = 8
PAD = 128

center_point = 5.0
half_width = 3.0
floor_estimate = 0.0
HIGHEST = lax.Precision.HIGHEST


def filter_coefficients():
    sigma_first = half_width / (floor_estimate - center_point)
    result = [(sigma_first / half_width, 0.0)]
    sigma_now = sigma_first
    for step in range(DEGREE - 1):
        sigma_next = 1.0 / (2.0 / sigma_first - sigma_now)
        result.append((2.0 * sigma_next / half_width, sigma_now * sigma_next))
        sigma_now = sigma_next
    return result


def at(slab, mode):
    return {"slab": slab, "mode": mode}


def remote(src, dst, send, recv, where):
    return pltpu.make_async_remote_copy(
        src_ref=src,
        dst_ref=dst,
        send_sem=send,
        recv_sem=recv,
        device_id=where,
        device_id_type=pl.DeviceIdType.MESH,
    )


def exchange(src, dst, send, recv, count, me, place):
    copies = []
    for j in range(1, count):
        peer = lax.rem(me + j, count)
        copy = remote(
            src(peer), dst(me), send.at[peer], recv.at[me], place(peer)
        )
        copy.start()
        copies.append(copy)
    return copies


def arrive(src, dst, send, recv, count, me, place):
    for j in range(1, count):
        peer = lax.rem(me + j, count)
        remote(src(peer), dst(peer), send.at[peer], recv.at[peer], place(peer)).wait_recv()


def gather_kernel(
    nz, ny, nm, coef_ref, block_ref, mask_ref, panel_ref,
    filt_ref, x_ref, g_ref,
    raw, halo, mraw, mhalo, pt, y, mf, part, rs, tmp, yb, tmpz, zb, tmpg,
    loc_sem, halo_s, halo_r, mask_s, mask_r, p_s, p_r, z_s, z_r, rs_s, rs_r, y_s, y_r, zz_s, zz_r, ag_s, ag_r, out_sem,
):
    ns = nz * ny
    slab = lax.axis_index("slab")
    m = lax.axis_index("mode")
    zi = slab // ny
    yi = lax.rem(slab, ny)
    mb, rows, cols = block_ref.shape
    wide = cols // nm
    up = lax.rem(slab + ns - 1, ns)
    down = lax.rem(slab + 1, ns)

    local = [pltpu.make_async_copy(mask_ref, mraw, loc_sem.at[2 * rows])]
    local += [pltpu.make_async_copy(block_ref.at[:, r, :], raw.at[r], loc_sem.at[r]) for r in range(rows)]
    local += [pltpu.make_async_copy(panel_ref.at[:, r, :], pt.at[r], loc_sem.at[rows + r]) for r in range(rows)]
    for copy in local:
        copy.start()

    barrier = pltpu.get_barrier_semaphore()

    def greet(where):
        pl.semaphore_signal(barrier, inc=1, device_id=where, device_id_type=pl.DeviceIdType.MESH)

    greet(at(up, m))
    greet(at(down, m))
    for j in range(1, nm):
        greet(at(slab, lax.rem(m + j, nm)))
    for j in range(1, ny):
        greet(at(zi * ny + lax.rem(yi + j, ny), m))
    for j in range(1, nz):
        greet(at(lax.rem(zi + j, nz) * ny + yi, m))
    for copy in local[: 1 + rows]:
        copy.wait()
    pl.semaphore_wait(barrier, 2 + nm - 1 + ny - 1 + nz - 1)

    sends = []
    to_down = remote(mraw, mhalo.at[0], mask_s.at[0], mask_r.at[0], at(down, m))
    to_up = remote(mraw, mhalo.at[1], mask_s.at[1], mask_r.at[1], at(up, m))
    mask_copies = [to_down, to_up]
    for copy in mask_copies:
        copy.start()
    halo_copies = [[], []]
    for d in range(1, rows + 1):
        lo, hi = rows - d, d - 1
        top = remote(raw.at[lo], halo.at[0, lo], halo_s.at[0, lo], halo_r.at[0, lo], at(down, m))
        bottom = remote(raw.at[hi], halo.at[1, hi], halo_s.at[1, hi], halo_r.at[1, hi], at(up, m))
        top.start()
        bottom.start()
        halo_copies[0].append(top)
        halo_copies[1].append(bottom)
    for copy in local[1 + rows:]:
        copy.wait()

    def mates(peer):
        return at(slab, peer)

    def along_y(peer):
        return at(zi * ny + peer, m)

    def along_z(peer):
        return at(peer * ny + yi, m)

    def columns(peer):
        return pl.ds(pl.multiple_of(peer * wide, wide), wide)

    def eight(peer, base=0):
        return pl.ds(pl.multiple_of(base + peer * mb, mb), mb)

    nmodes = nm * mb
    p_src = lambda peer: pt.at[:, :, columns(peer)]
    p_dst = lambda who: x_ref.at[:, eight(who, nmodes), :]
    sends += exchange(p_src, p_dst, p_s, p_r, nm, m, mates)
    x_ref[:, eight(m, nmodes), :] = pt[:, :, columns(m)]

    zero_pad = jnp.zeros((mb, PAD), jnp.float32)
    for r in range(rows):
        row = jnp.broadcast_to(mraw[r:r + 1, :].astype(jnp.float32), (mb, cols))
        mf[rows + r, :, :cols] = row
        mf[rows + r, :, cols:] = zero_pad
        y[0, rows + r, :, :cols] = raw[r] * row
        y[0, rows + r, :, cols:] = zero_pad

    def row_step(k, r):
        here = y[k - 1, r]
        total = here + y[k - 1, r - 1] + y[k - 1, r + 1]
        total = total + pltpu.roll(here, 1, 1) + pltpu.roll(here, cols + PAD - 1, 1)
        before = y[jnp.maximum(k - 2, 0), r]
        y[k, r] = mf[r] * (total * coef_ref[0, k]) - before * coef_ref[1, k]

    def stage(d):

        def body(k, carry):
            row_step(k, rows - d + k)
            row_step(k, 2 * rows - 1 + d - k)
            return carry

        lax.fori_loop(1, min(DEGREE, d + 3) + 1, body, 0)

    def inner(k, carry):
        def one(r, c):
            row_step(k, r)
            return c

        return lax.fori_loop(rows + k, 2 * rows - k, one, carry)

    lax.fori_loop(1, rows // 2, inner, 0)

    for copy in mask_copies:
        copy.wait_recv()
    inside = [jnp.where(slab > 0, 1.0, 0.0), jnp.where(slab < ns - 1, 1.0, 0.0)]
    for side in range(2):
        for r in range(rows):
            index = r if side == 0 else 2 * rows + r
            row = mhalo[side, r:r + 1, :].astype(jnp.float32) * inside[side]
            mf[index, :, :cols] = jnp.broadcast_to(row, (mb, cols))
            mf[index, :, cols:] = zero_pad

    z_src = lambda r: (lambda peer: y.at[DEGREE, rows + r, :, columns(peer)])
    z_dst = lambda r: (lambda who: x_ref.at[r, eight(who), :])
    done_rows = []
    for d in range(1, rows + 1):
        for side, r in ((0, rows - d), (1, d - 1)):
            halo_copies[side][d - 1].wait_recv()
            index = r if side == 0 else 2 * rows + r
            y[0, index, :, :cols] = halo[side, r] * mf[index, :, :cols]
            y[0, index, :, cols:] = zero_pad
        stage(d)
        if d > rows // 2:
            for r in (rows - d, d - 1):
                sends += exchange(z_src(r), z_dst(r), z_s.at[r], z_r.at[r], nm, m, mates)
                x_ref[r, eight(m), :] = y[DEGREE, rows + r, :, columns(m)]
                done_rows.append(r)

    outs = [
        pltpu.make_async_copy(y.at[DEGREE, rows + r, :, pl.ds(0, cols)], filt_ref.at[r], out_sem.at[r])
        for r in range(rows)
    ]
    for copy in outs:
        copy.start()

    def reduce_out(which):
        rs[which, m] = part[which, m]
        return exchange(
            lambda peer: part.at[which, peer], lambda who: rs.at[which, who],
            rs_s.at[which], rs_r.at[which], nm, m, mates,
        )

    def sum_and_send(which, from_buf, from_s, from_r, count, me, place, out, to_buf, to_s, to_r, to_count, to_me, to_place):
        arrive(lambda peer: out.at[which], lambda who: from_buf.at[which, who], from_s.at[which], from_r.at[which], count, me, place)
        total = from_buf[which, 0]
        for j in range(1, count):
            total = total + from_buf[which, j]
        out[which] = total
        to_buf[which, to_me] = total
        return exchange(
            lambda peer: out.at[which], lambda who: to_buf.at[which, who],
            to_s.at[which], to_r.at[which], to_count, to_me, to_place,
        )

    def to_y(which):
        return sum_and_send(which, rs, rs_s, rs_r, nm, m, mates, tmp, yb, y_s, y_r, ny, yi, along_y)

    def to_z(which):
        return sum_and_send(which, yb, y_s, y_r, ny, yi, along_y, tmpz, zb, zz_s, zz_r, nz, zi, along_z)

    def to_all(which):
        return sum_and_send(which, zb, zz_s, zz_r, nz, zi, along_z, tmpg, g_ref, ag_s, ag_r, nm, m, mates)

    def finish(which):
        arrive(lambda peer: tmpg.at[which], lambda who: g_ref.at[which, who], ag_s.at[which], ag_r.at[which], nm, m, mates)

    contract = (((1,), (1,)), ((), ()))
    arrive(p_src, p_dst, p_s, p_r, nm, m, mates)
    panel_part = jnp.zeros((nmodes, nmodes), jnp.float32)
    for r in range(rows):
        b = x_ref[r, nmodes:, :]
        panel_part += lax.dot_general(b, b, contract, precision=HIGHEST, preferred_element_type=jnp.float32)
    panel_part = jnp.concatenate([panel_part, jnp.zeros((nmodes, nmodes), jnp.float32)], axis=1)
    for j in range(nm):
        part[1, j] = panel_part[j * mb:(j + 1) * mb]
    sends += reduce_out(1)

    block_part = jnp.zeros((nmodes, 2 * nmodes), jnp.float32)
    for r in done_rows:
        arrive(z_src(r), z_dst(r), z_s.at[r], z_r.at[r], nm, m, mates)
        both = x_ref[r]
        block_part += lax.dot_general(
            both[:nmodes], both, contract, precision=HIGHEST, preferred_element_type=jnp.float32
        )
    for j in range(nm):
        part[0, j] = block_part[j * mb:(j + 1) * mb]
    sends += reduce_out(0)
    sends += to_y(1)
    sends += to_y(0)
    sends += to_z(1)
    sends += to_z(0)
    sends += to_all(1)
    sends += to_all(0)
    finish(1)
    finish(0)

    for copy in outs:
        copy.wait()
    for copy in sends + mask_copies + halo_copies[0] + halo_copies[1]:
        copy.wait_send()


def factor_kernel(n, mb, cells, g_ref, filt_ref, w_ref, out_ref, sem):
    rows = filt_ref.shape[0]
    outs = [pltpu.make_async_copy(filt_ref.at[r], out_ref.at[:, r, :], sem.at[r]) for r in range(rows)]
    for copy in outs:
        copy.start()
    nb = 2 * n // mb
    zeros = jnp.zeros((n, n), jnp.float32)
    top = g_ref[0].reshape(n, 2 * n)
    panel = g_ref[1].reshape(n, 2 * n)
    cross = top[:, n:]
    full = jnp.concatenate(
        [top, jnp.concatenate([cross.T, panel[:, :n]], axis=1)], axis=0
    )
    w_ref[...] = eliminate(full, n, mb, nb, cells)
    for copy in outs:
        copy.wait()


def eliminate(full, n, mb, nb, cells):
    width = 2 * n
    a = [full[i * mb:(i + 1) * mb] for i in range(nb)]
    lane = lax.broadcasted_iota(jnp.int32, (mb, width), 1)
    sub = lax.broadcasted_iota(jnp.int32, (mb, width), 0)
    result = []
    for b in range(nb):
        base = b * mb
        inside = (lane >= base) & (lane < base + mb)
        block = a[b]
        rowb = [jnp.broadcast_to(block[i:i + 1, :], (mb, width)) for i in range(mb)]
        e = [[jnp.broadcast_to(rowb[i][:, base + j:base + j + 1], (mb, width)) for j in range(i + 1)] for i in range(mb)]
        later = range(b + 1, nb)
        column = {
            i: [jnp.broadcast_to(a[i][:, base + k:base + k + 1], (mb, width)) for k in range(mb)] for i in later
        }
        row = [jnp.where(inside, jnp.where(lane == base + i, 1.0, 0.0), rowb[i]) for i in range(mb)]
        pivot, inverse = [], []
        f = [[None] * mb for _ in range(mb)]
        for k in range(mb):
            pivot.append(e[k][k])
            inverse.append(1.0 / e[k][k])
            for i in range(k + 1, mb):
                f[i][k] = e[i][k] * inverse[k]
            for i in range(k + 1, mb):
                for j in range(k + 1, i + 1):
                    e[i][j] = e[i][j] - f[i][k] * e[j][k]
                row[i] = row[i] - f[i][k] * row[k]
        if base >= n:
            scaled = jnp.zeros((mb, width), jnp.float32)
            for i in range(mb):
                scaled = jnp.where(sub == i, row[i] * lax.rsqrt(pivot[i] * (1.0 / cells)), scaled)
            result.append(jnp.where(lane < base + mb, scaled, 0.0))
        if b == nb - 1:
            break
        v = [row[i] * inverse[i] for i in range(mb)]
        for k in reversed(range(mb)):
            for i in range(k):
                v[i] = v[i] - f[k][i] * v[k]
        for i in later:
            total = column[i][0] * v[0]
            for k in range(1, mb):
                total = total + column[i][k] * v[k]
            a[i] = jnp.where(inside, 0.0, a[i]) - total
    return jnp.concatenate(result, axis=0)


def apply_kernel(nm, x_ref, w_ref, out_ref, mixed, send, recv):
    slab = lax.axis_index("slab")
    m = lax.axis_index("mode")
    rows, mb, cols = out_ref.shape
    wide = cols // nm
    barrier = pltpu.get_barrier_semaphore()
    for j in range(1, nm):
        pl.semaphore_signal(
            barrier, inc=1, device_id=at(slab, lax.rem(m + j, nm)), device_id_type=pl.DeviceIdType.MESH
        )
    pl.semaphore_wait(barrier, nm - 1)

    def columns(peer):
        return pl.ds(pl.multiple_of(peer * wide, wide), wide)

    def eight(peer):
        return pl.ds(pl.multiple_of(peer * mb, mb), mb)

    def mates(peer):
        return at(slab, peer)

    src = lambda r: (lambda peer: mixed.at[r, eight(peer), :])
    dst = lambda r: (lambda who: out_ref.at[r, :, columns(who)])
    w = w_ref[...]
    sends = []
    for r in range(rows):
        mixed[r] = jnp.dot(w, x_ref[r], precision=HIGHEST, preferred_element_type=jnp.float32)
        sends += exchange(src(r), dst(r), send.at[r], recv.at[r], nm, m, mates)
        out_ref[r, :, columns(m)] = mixed[r, eight(m), :]
    for r in range(rows):
        arrive(src(r), dst(r), send.at[r], recv.at[r], nm, m, mates)
    for copy in sends:
        copy.wait_send()


def shards(ns, nm, block_input, drum_mask, panel):
    ny = ROWS_Y if ns % ROWS_Y == 0 else 2
    nz = ns // ny
    mb, rows, cols = block_input.shape
    wide = cols // nm
    n = nm * mb
    f32 = jnp.float32
    pairs = filter_coefficients()
    coef = jnp.array(
        [[0.0] + [-first for first, _ in pairs], [0.0] + [second for _, second in pairs]], f32
    )
    vmem = pl.BlockSpec(memory_space=pltpu.VMEM)
    hbm = pl.BlockSpec(memory_space=pl.ANY)
    dma = pltpu.SemaphoreType.DMA
    filt, x, g = pl.pallas_call(
        functools.partial(gather_kernel, nz, ny, nm),
        out_shape=(
            jax.ShapeDtypeStruct((rows, mb, cols), f32),
            jax.ShapeDtypeStruct((rows, 2 * n, wide), f32),
            jax.ShapeDtypeStruct((2, nm, mb, 2 * n), f32),
        ),
        in_specs=[pl.BlockSpec(memory_space=pltpu.SMEM), hbm, hbm, hbm],
        out_specs=(hbm, vmem, vmem),
        scratch_shapes=[
            pltpu.VMEM((rows, mb, cols), f32),
            pltpu.VMEM((2, rows, mb, cols), f32),
            pltpu.VMEM((rows, cols), jnp.int32),
            pltpu.VMEM((2, rows, cols), jnp.int32),
            pltpu.VMEM((rows, mb, cols), f32),
            pltpu.VMEM((DEGREE + 1, 3 * rows, mb, cols + PAD), f32),
            pltpu.VMEM((3 * rows, mb, cols + PAD), f32),
            pltpu.VMEM((2, nm, mb, 2 * n), f32),
            pltpu.VMEM((2, nm, mb, 2 * n), f32),
            pltpu.VMEM((2, mb, 2 * n), f32),
            pltpu.VMEM((2, ny, mb, 2 * n), f32),
            pltpu.VMEM((2, mb, 2 * n), f32),
            pltpu.VMEM((2, nz, mb, 2 * n), f32),
            pltpu.VMEM((2, mb, 2 * n), f32),
            dma((2 * rows + 1,)),
            dma((2, rows)), dma((2, rows)),
            dma((2,)), dma((2,)),
            dma((nm,)), dma((nm,)),
            dma((rows, nm)), dma((rows, nm)),
            dma((2, nm)), dma((2, nm)),
            dma((2, ny)), dma((2, ny)),
            dma((2, nz)), dma((2, nz)),
            dma((2, nm)), dma((2, nm)),
            dma((rows,)),
        ],
        compiler_params=pltpu.CompilerParams(collective_id=0, has_side_effects=True),
        name="filter_gram",
    )(coef, block_input, drum_mask, panel)
    w, filtered = pl.pallas_call(
        functools.partial(factor_kernel, n, mb, float(ns * rows * cols)),
        out_shape=(
            jax.ShapeDtypeStruct((n, 2 * n), f32),
            jax.ShapeDtypeStruct((mb, rows, cols), f32),
        ),
        in_specs=[vmem, hbm],
        out_specs=(vmem, hbm),
        scratch_shapes=[dma((rows,))],
        name="factor",
    )(g, filt)
    spread = pl.pallas_call(
        functools.partial(apply_kernel, nm),
        out_shape=jax.ShapeDtypeStruct((rows, mb, cols), f32),
        in_specs=[vmem, vmem],
        out_specs=vmem,
        scratch_shapes=[
            pltpu.VMEM((rows, n, wide), f32),
            dma((rows, nm)), dma((rows, nm)),
        ],
        compiler_params=pltpu.CompilerParams(collective_id=1, has_side_effects=True),
        name="apply",
    )(x, w)
    return (filtered, jnp.transpose(spread, (1, 0, 2)))


def solution(mesh):
    placed = (P("mode", "slab", None), P("slab", None), P("mode", "slab", None))
    return jax.shard_map(
        functools.partial(shards, mesh.shape["slab"], mesh.shape["mode"]),
        mesh=mesh,
        in_specs=placed,
        out_specs=(P("mode", "slab", None), P("mode", "slab", None)),
        check_vma=False,
    )
```

```python
import functools

import jax
import jax.numpy as jnp
from jax import lax
from jax.experimental import pallas as pl
from jax.experimental.pallas import tpu as pltpu
from jax.sharding import PartitionSpec as P

DEGREE = 8
ROWS_Y = 8
PAD = 128
VMEM_LIMIT = 54000 << 10

center_point = 5.0
half_width = 3.0
floor_estimate = 0.0


def filter_coefficients():
    sigma_first = half_width / (floor_estimate - center_point)
    result = [(sigma_first / half_width, 0.0)]
    sigma_now = sigma_first
    for step in range(DEGREE - 1):
        sigma_next = 1.0 / (2.0 / sigma_first - sigma_now)
        result.append((2.0 * sigma_next / half_width, sigma_now * sigma_next))
        sigma_now = sigma_next
    return result


def at(slab, mode):
    return {"slab": slab, "mode": mode}


def remote(src, dst, send, recv, where):
    return pltpu.make_async_remote_copy(
        src_ref=src,
        dst_ref=dst,
        send_sem=send,
        recv_sem=recv,
        device_id=where,
        device_id_type=pl.DeviceIdType.MESH,
    )


def exchange(src, dst, send, recv, count, me, place):
    copies = []
    for j in range(1, count):
        peer = lax.rem(me + j, count)
        copy = remote(
            src(peer), dst(me), send.at[peer], recv.at[me], place(peer)
        )
        copy.start()
        copies.append(copy)
    return copies


def arrive(src, dst, send, recv, count, me, place):
    for j in range(1, count):
        peer = lax.rem(me + j, count)
        remote(src(peer), dst(peer), send.at[peer], recv.at[peer], place(peer)).wait_recv()


def pick(k, values):
    out = jnp.float32(values[0])
    for index in range(1, len(values)):
        out = jnp.where(k == index, jnp.float32(values[index]), out)
    return out


def halves(value):
    high = value.astype(jnp.bfloat16)
    return high, (value - high.astype(jnp.float32)).astype(jnp.bfloat16)


def whole_kernel(
    nz, ny, nm, cells, block_ref, mask_ref, panel_ref,
    filt_ref, spread_ref,
    raw, halo, mraw, mhalo, pt, y, mf, x, xs, part, rs, tmp, yb, tmpz, zb, tmpg, g, mixed,
    loc_sem, halo_s, halo_r, mask_s, mask_r, p_s, p_r, z_s, z_r, rs_s, rs_r, y_s, y_r, zz_s, zz_r, ag_s, ag_r,
    back_s, back_r, out_sem,
):
    ns = nz * ny
    slab = lax.axis_index("slab")
    m = lax.axis_index("mode")
    zi = slab // ny
    yi = lax.rem(slab, ny)
    mb, rows, cols = block_ref.shape
    wide = cols // nm
    n = nm * mb
    up = lax.rem(slab + ns - 1, ns)
    down = lax.rem(slab + 1, ns)
    pairs = filter_coefficients()
    gain = [0.0] + [-first for first, _ in pairs]
    drag = [0.0] + [second for _, second in pairs]

    local = [pltpu.make_async_copy(mask_ref, mraw, loc_sem.at[2 * rows])]
    local += [pltpu.make_async_copy(block_ref.at[:, r, :], raw.at[r], loc_sem.at[r]) for r in range(rows)]
    local += [pltpu.make_async_copy(panel_ref.at[:, r, :], pt.at[r], loc_sem.at[rows + r]) for r in range(rows)]
    for copy in local:
        copy.start()

    barrier = pltpu.get_barrier_semaphore()

    def greet(where):
        pl.semaphore_signal(barrier, inc=1, device_id=where, device_id_type=pl.DeviceIdType.MESH)

    greet(at(up, m))
    greet(at(down, m))
    for j in range(1, nm):
        greet(at(slab, lax.rem(m + j, nm)))
    for j in range(1, ny):
        greet(at(zi * ny + lax.rem(yi + j, ny), m))
    for j in range(1, nz):
        greet(at(lax.rem(zi + j, nz) * ny + yi, m))
    for copy in local[: 1 + rows]:
        copy.wait()
    pl.semaphore_wait(barrier, 2 + nm - 1 + ny - 1 + nz - 1)

    sends = []
    mask_copies = [
        remote(mraw, mhalo.at[0], mask_s.at[0], mask_r.at[0], at(down, m)),
        remote(mraw, mhalo.at[1], mask_s.at[1], mask_r.at[1], at(up, m)),
    ]
    for copy in mask_copies:
        copy.start()
    halo_copies = [[], []]
    for d in range(1, rows + 1):
        lo, hi = rows - d, d - 1
        top = remote(raw.at[lo], halo.at[0, lo], halo_s.at[0, lo], halo_r.at[0, lo], at(down, m))
        bottom = remote(raw.at[hi], halo.at[1, hi], halo_s.at[1, hi], halo_r.at[1, hi], at(up, m))
        top.start()
        bottom.start()
        halo_copies[0].append(top)
        halo_copies[1].append(bottom)
    for copy in local[1 + rows:]:
        copy.wait()

    def mates(peer):
        return at(slab, peer)

    def along_y(peer):
        return at(zi * ny + peer, m)

    def along_z(peer):
        return at(peer * ny + yi, m)

    def columns(peer):
        return pl.ds(pl.multiple_of(peer * wide, wide), wide)

    def eight(peer, base=0):
        return pl.ds(pl.multiple_of(base + peer * mb, mb), mb)

    p_src = lambda peer: pt.at[:, :, columns(peer)]
    p_dst = lambda who: x.at[:, eight(who, n), :]
    sends += exchange(p_src, p_dst, p_s, p_r, nm, m, mates)
    x[:, eight(m, n), :] = pt[:, :, columns(m)]

    zero_pad = jnp.zeros((mb, PAD), jnp.float32)
    for r in range(rows):
        row = jnp.broadcast_to(mraw[r:r + 1, :].astype(jnp.float32), (mb, cols))
        mf[rows + r, :, :cols] = row
        mf[rows + r, :, cols:] = zero_pad
        y[0, rows + r, :, :cols] = raw[r] * row
        y[0, rows + r, :, cols:] = zero_pad

    def row_step(k, r):
        here = y[k - 1, r]
        total = here + y[k - 1, r - 1] + y[k - 1, r + 1]
        total = total + pltpu.roll(here, 1, 1) + pltpu.roll(here, cols + PAD - 1, 1)
        before = y[jnp.maximum(k - 2, 0), r]
        y[k, r] = mf[r] * (total * pick(k, gain)) - before * pick(k, drag)

    def stage(d):
        def body(k, carry):
            row_step(k, rows - d + k)
            row_step(k, 2 * rows - 1 + d - k)
            return carry

        lax.fori_loop(1, min(DEGREE, d + 3) + 1, body, 0)

    def inner(k, carry):
        def one(r, c):
            row_step(k, r)
            return c

        return lax.fori_loop(rows + k, 2 * rows - k, one, carry)

    lax.fori_loop(1, rows // 2, inner, 0)

    for copy in mask_copies:
        copy.wait_recv()
    inside = [jnp.where(slab > 0, 1.0, 0.0), jnp.where(slab < ns - 1, 1.0, 0.0)]
    for side in range(2):
        for r in range(rows):
            index = r if side == 0 else 2 * rows + r
            row = mhalo[side, r:r + 1, :].astype(jnp.float32) * inside[side]
            mf[index, :, :cols] = jnp.broadcast_to(row, (mb, cols))
            mf[index, :, cols:] = zero_pad

    z_src = lambda r: (lambda peer: y.at[DEGREE, rows + r, :, columns(peer)])
    z_dst = lambda r: (lambda who: x.at[r, eight(who), :])
    contract = (((1,), (1,)), ((), ()))

    def products(left, right):
        return lax.dot_general(left, right, contract, preferred_element_type=jnp.float32)

    def panel_gram(r):
        high, low = halves(x[r, n:, :])
        xs[r, n:2 * n, :] = high
        xs[r, 3 * n:, :] = low
        mixed_part = products(high, low)
        return products(high, high) + products(low, low), mixed_part

    def block_gram(r):
        arrive(z_src(r), z_dst(r), z_s.at[r], z_r.at[r], nm, m, mates)
        high, low = halves(x[r, :n, :])
        xs[r, :n, :] = high
        xs[r, 2 * n:3 * n, :] = low
        all_high, all_low = xs[r, :2 * n, :], xs[r, 2 * n:, :]
        return (
            products(high, all_high) + products(low, all_low) + products(high, all_low) + products(low, all_high)
        )

    def reduce_out(which):
        rs[which, m] = part[which, m]
        return exchange(
            lambda peer: part.at[which, peer], lambda who: rs.at[which, who],
            rs_s.at[which], rs_r.at[which], nm, m, mates,
        )

    panel_part = jnp.zeros((n, n), jnp.float32)
    panel_mixed = jnp.zeros((n, n), jnp.float32)
    block_part = jnp.zeros((n, 2 * n), jnp.float32)
    quarter = rows // 4
    panel_rows = {
        rows - 3: list(range(quarter, rows - quarter)),
        rows - 2: list(range(quarter)) + list(range(rows - quarter, rows)),
    }
    outs = []
    for d in range(1, rows + 1):
        for side, r in ((0, rows - d), (1, d - 1)):
            halo_copies[side][d - 1].wait_recv()
            index = r if side == 0 else 2 * rows + r
            y[0, index, :, :cols] = halo[side, r] * mf[index, :, :cols]
            y[0, index, :, cols:] = zero_pad
        stage(d)
        if d > rows // 2:
            for r in (rows - d, d - 1):
                sends += exchange(z_src(r), z_dst(r), z_s.at[r], z_r.at[r], nm, m, mates)
                x[r, eight(m), :] = y[DEGREE, rows + r, :, columns(m)]
                out = pltpu.make_async_copy(y.at[DEGREE, rows + r, :, pl.ds(0, cols)], filt_ref.at[r], out_sem.at[r])
                out.start()
                outs.append(out)
        if d in panel_rows:
            if d == rows - 3:
                arrive(p_src, p_dst, p_s, p_r, nm, m, mates)
            for r in panel_rows[d]:
                same, cross = panel_gram(r)
                panel_part += same
                panel_mixed += cross
        if d == rows - 2:
            panel_all = panel_part + panel_mixed + panel_mixed.T
            panel_all = jnp.concatenate([panel_all, jnp.zeros((n, n), jnp.float32)], axis=1)
            for j in range(nm):
                part[1, j] = panel_all[j * mb:(j + 1) * mb]
            sends += reduce_out(1)
        if d > rows // 2 + 1:
            for r in (rows - d + 1, d - 2):
                block_part += block_gram(r)

    def sum_and_send(which, from_buf, from_s, from_r, count, me, place, out, to_buf, to_s, to_r, to_count, to_me, to_place):
        arrive(lambda peer: out.at[which], lambda who: from_buf.at[which, who], from_s.at[which], from_r.at[which], count, me, place)
        total = from_buf[which, 0]
        for j in range(1, count):
            total = total + from_buf[which, j]
        out[which] = total
        to_buf[which, to_me] = total
        return exchange(
            lambda peer: out.at[which], lambda who: to_buf.at[which, who],
            to_s.at[which], to_r.at[which], to_count, to_me, to_place,
        )

    def to_y(which):
        return sum_and_send(which, rs, rs_s, rs_r, nm, m, mates, tmp, yb, y_s, y_r, ny, yi, along_y)

    def to_z(which):
        return sum_and_send(which, yb, y_s, y_r, ny, yi, along_y, tmpz, zb, zz_s, zz_r, nz, zi, along_z)

    def to_all(which):
        return sum_and_send(which, zb, zz_s, zz_r, nz, zi, along_z, tmpg, g, ag_s, ag_r, nm, m, mates)

    def finish(which):
        arrive(lambda peer: tmpg.at[which], lambda who: g.at[which, who], ag_s.at[which], ag_r.at[which], nm, m, mates)

    for r in (0, rows - 1):
        block_part += block_gram(r)
    for j in range(nm):
        part[0, j] = block_part[j * mb:(j + 1) * mb]
    sends += reduce_out(0)
    sends += to_y(1)
    sends += to_y(0)
    sends += to_z(1)
    sends += to_z(0)
    sends += to_all(1)
    sends += to_all(0)
    finish(1)
    finish(0)

    top = g[0].reshape(n, 2 * n)
    panel = g[1].reshape(n, 2 * n)
    full = jnp.concatenate(
        [top, jnp.concatenate([top[:, n:].T, panel[:, :n]], axis=1)], axis=0
    )
    w_high, w_low = halves(eliminate(full, n, mb, 2 * n // mb, cells))
    back_src = lambda r: (lambda peer: mixed.at[r, eight(peer), :])
    back_dst = lambda r: (lambda who: spread_ref.at[r, :, columns(who)])
    for r in range(rows):
        high, low = xs[r, :2 * n, :], xs[r, 2 * n:, :]
        mixed[r] = (
            jnp.dot(w_high, high, preferred_element_type=jnp.float32)
            + jnp.dot(w_high, low, preferred_element_type=jnp.float32)
            + jnp.dot(w_low, high, preferred_element_type=jnp.float32)
        )
        sends += exchange(back_src(r), back_dst(r), back_s.at[r], back_r.at[r], nm, m, mates)
        spread_ref[r, :, columns(m)] = mixed[r, eight(m), :]
    for r in range(rows):
        arrive(back_src(r), back_dst(r), back_s.at[r], back_r.at[r], nm, m, mates)

    for copy in outs:
        copy.wait()
    for copy in sends + mask_copies + halo_copies[0] + halo_copies[1]:
        copy.wait_send()


def eliminate(full, n, mb, nb, cells):
    width = 2 * n
    a = [full[i * mb:(i + 1) * mb] for i in range(nb)]
    lane = lax.broadcasted_iota(jnp.int32, (mb, width), 1)
    sub = lax.broadcasted_iota(jnp.int32, (mb, width), 0)
    result = []
    for b in range(nb):
        base = b * mb
        inside = (lane >= base) & (lane < base + mb)
        block = a[b]
        rowb = [jnp.broadcast_to(block[i:i + 1, :], (mb, width)) for i in range(mb)]
        e = [[jnp.broadcast_to(rowb[i][:, base + j:base + j + 1], (mb, width)) for j in range(i + 1)] for i in range(mb)]
        later = range(b + 1, nb)
        column = {
            i: [jnp.broadcast_to(a[i][:, base + k:base + k + 1], (mb, width)) for k in range(mb)] for i in later
        }
        row = [jnp.where(inside, jnp.where(lane == base + i, 1.0, 0.0), rowb[i]) for i in range(mb)]
        pivot, inverse = [], []
        f = [[None] * mb for _ in range(mb)]
        for k in range(mb):
            pivot.append(e[k][k])
            inverse.append(1.0 / e[k][k])
            for i in range(k + 1, mb):
                f[i][k] = e[i][k] * inverse[k]
            for i in range(k + 1, mb):
                for j in range(k + 1, i + 1):
                    e[i][j] = e[i][j] - f[i][k] * e[j][k]
                row[i] = row[i] - f[i][k] * row[k]
        if base >= n:
            scaled = jnp.zeros((mb, width), jnp.float32)
            for i in range(mb):
                scaled = jnp.where(sub == i, row[i] * lax.rsqrt(pivot[i] * (1.0 / cells)), scaled)
            result.append(jnp.where(lane < base + mb, scaled, 0.0))
        if b == nb - 1:
            break
        v = [row[i] * inverse[i] for i in range(mb)]
        for k in reversed(range(mb)):
            for i in range(k):
                v[i] = v[i] - f[k][i] * v[k]
        for i in later:
            total = column[i][0] * v[0]
            for k in range(1, mb):
                total = total + column[i][k] * v[k]
            a[i] = jnp.where(inside, 0.0, a[i]) - total
    return jnp.concatenate(result, axis=0)


def place_kernel(filt_ref, spread_ref, filtered_ref, orthonormal_ref, sem):
    copies = []
    for r in range(filt_ref.shape[0]):
        copies.append(pltpu.make_async_copy(filt_ref.at[r], filtered_ref.at[:, r, :], sem.at[0, r]))
        copies.append(pltpu.make_async_copy(spread_ref.at[r], orthonormal_ref.at[:, r, :], sem.at[1, r]))
    for copy in copies:
        copy.start()
    for copy in copies:
        copy.wait()


def shards(ns, nm, block_input, drum_mask, panel):
    ny = ROWS_Y if ns % ROWS_Y == 0 else 2
    nz = ns // ny
    mb, rows, cols = block_input.shape
    wide = cols // nm
    n = nm * mb
    f32 = jnp.float32
    vmem = pl.BlockSpec(memory_space=pltpu.VMEM)
    hbm = pl.BlockSpec(memory_space=pl.ANY)
    dma = pltpu.SemaphoreType.DMA
    filt, spread = pl.pallas_call(
        functools.partial(whole_kernel, nz, ny, nm, float(ns * rows * cols)),
        out_shape=(
            jax.ShapeDtypeStruct((rows, mb, cols), f32),
            jax.ShapeDtypeStruct((rows, mb, cols), f32),
        ),
        in_specs=[hbm, hbm, hbm],
        out_specs=(hbm, vmem),
        scratch_shapes=[
            pltpu.VMEM((rows, mb, cols), f32),
            pltpu.VMEM((2, rows, mb, cols), f32),
            pltpu.VMEM((rows, cols), jnp.int32),
            pltpu.VMEM((2, rows, cols), jnp.int32),
            pltpu.VMEM((rows, mb, cols), f32),
            pltpu.VMEM((DEGREE + 1, 3 * rows, mb, cols + PAD), f32),
            pltpu.VMEM((3 * rows, mb, cols + PAD), f32),
            pltpu.VMEM((rows, 2 * n, wide), f32),
            pltpu.VMEM((rows, 4 * n, wide), jnp.bfloat16),
            pltpu.VMEM((2, nm, mb, 2 * n), f32),
            pltpu.VMEM((2, nm, mb, 2 * n), f32),
            pltpu.VMEM((2, mb, 2 * n), f32),
            pltpu.VMEM((2, ny, mb, 2 * n), f32),
            pltpu.VMEM((2, mb, 2 * n), f32),
            pltpu.VMEM((2, nz, mb, 2 * n), f32),
            pltpu.VMEM((2, mb, 2 * n), f32),
            pltpu.VMEM((2, nm, mb, 2 * n), f32),
            pltpu.VMEM((rows, n, wide), f32),
            dma((2 * rows + 1,)),
            dma((2, rows)), dma((2, rows)),
            dma((2,)), dma((2,)),
            dma((nm,)), dma((nm,)),
            dma((rows, nm)), dma((rows, nm)),
            dma((2, nm)), dma((2, nm)),
            dma((2, ny)), dma((2, ny)),
            dma((2, nz)), dma((2, nz)),
            dma((2, nm)), dma((2, nm)),
            dma((rows, nm)), dma((rows, nm)),
            dma((rows,)),
        ],
        compiler_params=pltpu.CompilerParams(
            collective_id=0, has_side_effects=True, vmem_limit_bytes=VMEM_LIMIT
        ),
        name="whole",
    )(block_input, drum_mask, panel)
    shape = jax.ShapeDtypeStruct((mb, rows, cols), f32)
    return pl.pallas_call(
        place_kernel,
        out_shape=(shape, shape),
        in_specs=[vmem, vmem],
        out_specs=(hbm, hbm),
        scratch_shapes=[dma((2, rows))],
        compiler_params=pltpu.CompilerParams(vmem_limit_bytes=8 << 20),
        name="place",
    )(filt, spread)


def solution(mesh):
    placed = (P("mode", "slab", None), P("slab", None), P("mode", "slab", None))
    return jax.shard_map(
        functools.partial(shards, mesh.shape["slab"], mesh.shape["mode"]),
        mesh=mesh,
        in_specs=placed,
        out_specs=(P("mode", "slab", None), P("mode", "slab", None)),
        check_vma=False,
    )
```

```python
import functools

import jax
import jax.numpy as jnp
from jax import lax
from jax.experimental import pallas as pl
from jax.experimental.pallas import tpu as pltpu
from jax.sharding import PartitionSpec as P

DEGREE = 8
ROWS_Y = 8
PAD = 128
VMEM_LIMIT = 54000 << 10

center_point = 5.0
half_width = 3.0
floor_estimate = 0.0


def filter_coefficients():
    sigma_first = half_width / (floor_estimate - center_point)
    result = [(sigma_first / half_width, 0.0)]
    sigma_now = sigma_first
    for step in range(DEGREE - 1):
        sigma_next = 1.0 / (2.0 / sigma_first - sigma_now)
        result.append((2.0 * sigma_next / half_width, sigma_now * sigma_next))
        sigma_now = sigma_next
    return result


def at(slab, mode):
    return {"slab": slab, "mode": mode}


def remote(src, dst, send, recv, where):
    return pltpu.make_async_remote_copy(
        src_ref=src,
        dst_ref=dst,
        send_sem=send,
        recv_sem=recv,
        device_id=where,
        device_id_type=pl.DeviceIdType.MESH,
    )


def exchange(src, dst, send, recv, count, me, place):
    copies = []
    for j in range(1, count):
        peer = lax.rem(me + j, count)
        copy = remote(
            src(peer), dst(me), send.at[peer], recv.at[me], place(peer)
        )
        copy.start()
        copies.append(copy)
    return copies


def arrive(src, dst, send, recv, count, me, place):
    for j in range(1, count):
        peer = lax.rem(me + j, count)
        remote(src(peer), dst(peer), send.at[peer], recv.at[peer], place(peer)).wait_recv()


def halves(value):
    high = value.astype(jnp.bfloat16)
    return high, (value - high.astype(jnp.float32)).astype(jnp.bfloat16)


def whole_kernel(
    nz, ny, nm, cells, block_ref, mask_ref, panel_ref,
    filt_ref, spread_ref,
    raw, halo, mraw, mhalo, pt, y0, y1, y2, y3, y4, y5, y6, y7, y8, mf, x, xs, part, rs, tmp, yb, tmpz, zb, tmpg, g, mixed,
    loc_sem, halo_s, halo_r, mask_s, mask_r, pass_s, pass_r, p_s, p_r, z_s, z_r, rs_s, rs_r, y_s, y_r, zz_s, zz_r, ag_s, ag_r,
    back_s, back_r, out_sem,
):
    ns = nz * ny
    slab = lax.axis_index("slab")
    m = lax.axis_index("mode")
    zi = slab // ny
    yi = lax.rem(slab, ny)
    mb, rows, cols = block_ref.shape
    wide = cols // nm
    n = nm * mb
    up = lax.rem(slab + ns - 1, ns)
    down = lax.rem(slab + 1, ns)
    y = [y0, y1, y2, y3, y4, y5, y6, y7, y8]
    pairs = filter_coefficients()
    scale = [1.0]
    for first, _ in pairs:
        scale.append(-first * scale[-1])
    drag = [0.0, 0.0] + [pairs[k - 1][1] * scale[k - 2] / scale[k] for k in range(2, DEGREE + 1)]
    last = DEGREE

    local = [pltpu.make_async_copy(mask_ref, mraw, loc_sem.at[2 * rows])]
    local += [pltpu.make_async_copy(block_ref.at[:, r, :], raw.at[r], loc_sem.at[r]) for r in range(rows)]
    local += [pltpu.make_async_copy(panel_ref.at[:, r, :], pt.at[r], loc_sem.at[rows + r]) for r in range(rows)]
    for copy in local:
        copy.start()

    barrier = pltpu.get_barrier_semaphore()

    def greet(where):
        pl.semaphore_signal(barrier, inc=1, device_id=where, device_id_type=pl.DeviceIdType.MESH)

    greet(at(up, m))
    greet(at(down, m))
    for j in range(1, nm):
        greet(at(slab, lax.rem(m + j, nm)))
    for j in range(1, ny):
        greet(at(zi * ny + lax.rem(yi + j, ny), m))
    for j in range(1, nz):
        greet(at(lax.rem(zi + j, nz) * ny + yi, m))
    for copy in local[: 1 + rows]:
        copy.wait()
    pl.semaphore_wait(barrier, 2 + nm - 1 + ny - 1 + nz - 1)

    sends = []
    core = lax.rem(m, 2)
    other = m + 1 - 2 * core
    half = pl.ds(pl.multiple_of(core * (cols // 2), 128), cols // 2)
    rest = pl.ds(pl.multiple_of((1 - core) * (cols // 2), 128), cols // 2)
    mask_copies = [
        remote(mraw.at[:, half], mhalo.at[0, :, half], mask_s.at[0], mask_r.at[0], at(down, m)),
        remote(mraw.at[:, half], mhalo.at[1, :, half], mask_s.at[1], mask_r.at[1], at(up, m)),
    ]
    mask_passes = [
        remote(mhalo.at[side, :, half], mhalo.at[side, :, half], pass_s.at[side], pass_r.at[side], at(slab, other))
        for side in range(2)
    ]
    mask_lands = [
        remote(mhalo.at[side, :, rest], mhalo.at[side, :, rest], pass_s.at[side], pass_r.at[side], at(slab, other))
        for side in range(2)
    ]
    for copy in mask_copies:
        copy.start()
    halo_copies = [[], []]
    for d in range(1, rows + 1):
        lo, hi = rows - d, d - 1
        top = remote(raw.at[lo], halo.at[0, lo], halo_s.at[0, lo], halo_r.at[0, lo], at(down, m))
        bottom = remote(raw.at[hi], halo.at[1, hi], halo_s.at[1, hi], halo_r.at[1, hi], at(up, m))
        top.start()
        bottom.start()
        halo_copies[0].append(top)
        halo_copies[1].append(bottom)
    for copy in local[1 + rows:]:
        copy.wait()

    def mates(peer):
        return at(slab, peer)

    def along_y(peer):
        return at(zi * ny + peer, m)

    def along_z(peer):
        return at(peer * ny + yi, m)

    def columns(peer):
        return pl.ds(pl.multiple_of(peer * wide, wide), wide)

    def eight(peer, base=0):
        return pl.ds(pl.multiple_of(base + peer * mb, mb), mb)

    p_src = lambda peer: pt.at[:, :, columns(peer)]
    p_dst = lambda who: x.at[:, eight(who, n), :]
    sends += exchange(p_src, p_dst, p_s, p_r, nm, m, mates)
    x[:, eight(m, n), :] = pt[:, :, columns(m)]

    zero_pad = jnp.zeros((mb, PAD), jnp.float32)
    for r in range(rows):
        row = jnp.broadcast_to(mraw[r:r + 1, :].astype(jnp.float32), (mb, cols))
        mf[rows + r, :, :cols] = row
        mf[rows + r, :, cols:] = zero_pad
        y0[rows + r, :, :cols] = raw[r] * row
        y0[rows + r, :, cols:] = zero_pad

    def row_step(k, r):
        here = y[k - 1][r]
        total = here + y[k - 1][r - 1] + y[k - 1][r + 1]
        total = total + pltpu.roll(here, 1, 1) + pltpu.roll(here, cols + PAD - 1, 1)
        new = mf[r] * total
        if k > 1:
            new = new - y[k - 2][r] * drag[k]
        y[k][r] = new * scale[k] if k == last else new

    def stage(d):
        for k in range(1, min(last, d + 3) + 1):
            row_step(k, rows - d + k)
            row_step(k, 2 * rows - 1 + d - k)

    for k in range(1, rows // 2):
        for r in range(rows + k, 2 * rows - k):
            row_step(k, r)

    for side in range(2):
        mask_copies[side].wait_recv()
        mask_passes[side].start()
    for copy in mask_lands:
        copy.wait_recv()
    inside = [jnp.where(slab > 0, 1.0, 0.0), jnp.where(slab < ns - 1, 1.0, 0.0)]
    for side in range(2):
        for r in range(rows):
            index = r if side == 0 else 2 * rows + r
            row = mhalo[side, r:r + 1, :].astype(jnp.float32) * inside[side]
            mf[index, :, :cols] = jnp.broadcast_to(row, (mb, cols))
            mf[index, :, cols:] = zero_pad

    z_src = lambda r: (lambda peer: y8.at[rows + r, :, columns(peer)])
    z_dst = lambda r: (lambda who: x.at[r, eight(who), :])
    contract = (((1,), (1,)), ((), ()))

    def products(left, right):
        return lax.dot_general(left, right, contract, preferred_element_type=jnp.float32)

    def panel_gram(r):
        high, low = halves(x[r, n:, :])
        xs[r, n:2 * n, :] = high
        xs[r, 3 * n:, :] = low
        mixed_part = products(high, low)
        return products(high, high) + products(low, low), mixed_part

    def block_gram(r):
        arrive(z_src(r), z_dst(r), z_s.at[r], z_r.at[r], nm, m, mates)
        high, low = halves(x[r, :n, :])
        xs[r, :n, :] = high
        xs[r, 2 * n:3 * n, :] = low
        all_high, all_low = xs[r, :2 * n, :], xs[r, 2 * n:, :]
        return (
            products(high, all_high) + products(low, all_low) + products(high, all_low) + products(low, all_high)
        )

    def reduce_out(which):
        rs[which, m] = part[which, m]
        return exchange(
            lambda peer: part.at[which, peer], lambda who: rs.at[which, who],
            rs_s.at[which], rs_r.at[which], nm, m, mates,
        )

    panel_part = jnp.zeros((n, n), jnp.float32)
    panel_mixed = jnp.zeros((n, n), jnp.float32)
    block_part = jnp.zeros((n, 2 * n), jnp.float32)
    quarter = rows // 4
    panel_rows = {
        rows - 3: list(range(quarter, rows - quarter)),
        rows - 2: list(range(quarter)) + list(range(rows - quarter, rows)),
    }
    outs = []
    for d in range(1, rows + 1):
        for side, r in ((0, rows - d), (1, d - 1)):
            halo_copies[side][d - 1].wait_recv()
            index = r if side == 0 else 2 * rows + r
            y0[index, :, :cols] = halo[side, r] * mf[index, :, :cols]
            y0[index, :, cols:] = zero_pad
        stage(d)
        if d > rows // 2:
            for r in (rows - d, d - 1):
                sends += exchange(z_src(r), z_dst(r), z_s.at[r], z_r.at[r], nm, m, mates)
                x[r, eight(m), :] = y8[rows + r, :, columns(m)]
                out = pltpu.make_async_copy(y8.at[rows + r, :, pl.ds(0, cols)], filt_ref.at[r], out_sem.at[r])
                out.start()
                outs.append(out)
        if d in panel_rows:
            if d == rows - 3:
                arrive(p_src, p_dst, p_s, p_r, nm, m, mates)
            for r in panel_rows[d]:
                same, cross = panel_gram(r)
                panel_part += same
                panel_mixed += cross
        if d == rows - 2:
            panel_all = panel_part + panel_mixed + panel_mixed.T
            panel_all = jnp.concatenate([panel_all, jnp.zeros((n, n), jnp.float32)], axis=1)
            for j in range(nm):
                part[1, j] = panel_all[j * mb:(j + 1) * mb]
            sends += reduce_out(1)
        if d > rows // 2 + 1:
            for r in (rows - d + 1, d - 2):
                block_part += block_gram(r)

    def sum_and_send(which, from_buf, from_s, from_r, count, me, place, out, to_buf, to_s, to_r, to_count, to_me, to_place):
        arrive(lambda peer: out.at[which], lambda who: from_buf.at[which, who], from_s.at[which], from_r.at[which], count, me, place)
        total = from_buf[which, 0]
        for j in range(1, count):
            total = total + from_buf[which, j]
        out[which] = total
        to_buf[which, to_me] = total
        return exchange(
            lambda peer: out.at[which], lambda who: to_buf.at[which, who],
            to_s.at[which], to_r.at[which], to_count, to_me, to_place,
        )

    def to_y(which):
        return sum_and_send(which, rs, rs_s, rs_r, nm, m, mates, tmp, yb, y_s, y_r, ny, yi, along_y)

    def to_z(which):
        return sum_and_send(which, yb, y_s, y_r, ny, yi, along_y, tmpz, zb, zz_s, zz_r, nz, zi, along_z)

    def to_all(which):
        return sum_and_send(which, zb, zz_s, zz_r, nz, zi, along_z, tmpg, g, ag_s, ag_r, nm, m, mates)

    def finish(which):
        arrive(lambda peer: tmpg.at[which], lambda who: g.at[which, who], ag_s.at[which], ag_r.at[which], nm, m, mates)

    for r in (0, rows - 1):
        block_part += block_gram(r)
    for j in range(nm):
        part[0, j] = block_part[j * mb:(j + 1) * mb]
    sends += reduce_out(0)
    sends += to_y(1)
    sends += to_y(0)
    sends += to_z(1)
    sends += to_z(0)
    sends += to_all(1)
    sends += to_all(0)
    finish(1)
    finish(0)

    top = g[0].reshape(n, 2 * n)
    panel = g[1].reshape(n, 2 * n)
    full = jnp.concatenate(
        [top, jnp.concatenate([top[:, n:].T, panel[:, :n]], axis=1)], axis=0
    )
    w_high, w_low = halves(eliminate(full, n, mb, 2 * n // mb, cells))
    back_src = lambda r: (lambda peer: mixed.at[r, eight(peer), :])
    back_dst = lambda r: (lambda who: spread_ref.at[r, :, columns(who)])
    for r in range(rows):
        high, low = xs[r, :2 * n, :], xs[r, 2 * n:, :]
        mixed[r] = (
            jnp.dot(w_high, high, preferred_element_type=jnp.float32)
            + jnp.dot(w_high, low, preferred_element_type=jnp.float32)
            + jnp.dot(w_low, high, preferred_element_type=jnp.float32)
        )
        sends += exchange(back_src(r), back_dst(r), back_s.at[r], back_r.at[r], nm, m, mates)
        spread_ref[r, :, columns(m)] = mixed[r, eight(m), :]
    for r in range(rows):
        arrive(back_src(r), back_dst(r), back_s.at[r], back_r.at[r], nm, m, mates)

    for copy in outs:
        copy.wait()
    for copy in sends + mask_copies + mask_passes + halo_copies[0] + halo_copies[1]:
        copy.wait_send()


def eliminate(full, n, mb, nb, cells):
    width = 2 * n
    a = [full[i * mb:(i + 1) * mb] for i in range(nb)]
    lane = lax.broadcasted_iota(jnp.int32, (mb, width), 1)
    sub = lax.broadcasted_iota(jnp.int32, (mb, width), 0)
    result = []
    for b in range(nb):
        base = b * mb
        inside = (lane >= base) & (lane < base + mb)
        block = a[b]
        rowb = [jnp.broadcast_to(block[i:i + 1, :], (mb, width)) for i in range(mb)]
        e = [[jnp.broadcast_to(rowb[i][:, base + j:base + j + 1], (mb, width)) for j in range(i + 1)] for i in range(mb)]
        later = range(b + 1, nb)
        column = {
            i: [jnp.broadcast_to(a[i][:, base + k:base + k + 1], (mb, width)) for k in range(mb)] for i in later
        }
        row = [jnp.where(inside, jnp.where(lane == base + i, 1.0, 0.0), rowb[i]) for i in range(mb)]
        pivot, inverse = [], []
        f = [[None] * mb for _ in range(mb)]
        for k in range(mb):
            pivot.append(e[k][k])
            inverse.append(1.0 / e[k][k])
            for i in range(k + 1, mb):
                f[i][k] = e[i][k] * inverse[k]
            for i in range(k + 1, mb):
                for j in range(k + 1, i + 1):
                    e[i][j] = e[i][j] - f[i][k] * e[j][k]
                row[i] = row[i] - f[i][k] * row[k]
        if base >= n:
            scaled = jnp.zeros((mb, width), jnp.float32)
            for i in range(mb):
                scaled = jnp.where(sub == i, row[i] * lax.rsqrt(pivot[i] * (1.0 / cells)), scaled)
            result.append(jnp.where(lane < base + mb, scaled, 0.0))
        if b == nb - 1:
            break
        v = [row[i] * inverse[i] for i in range(mb)]
        for k in reversed(range(mb)):
            for i in range(k):
                v[i] = v[i] - f[k][i] * v[k]
        for i in later:
            total = column[i][0] * v[0]
            for k in range(1, mb):
                total = total + column[i][k] * v[k]
            a[i] = jnp.where(inside, 0.0, a[i]) - total
    return jnp.concatenate(result, axis=0)


def place_kernel(filt_ref, spread_ref, filtered_ref, orthonormal_ref, sem):
    copies = []
    for r in range(filt_ref.shape[0]):
        copies.append(pltpu.make_async_copy(filt_ref.at[r], filtered_ref.at[:, r, :], sem.at[0, r]))
        copies.append(pltpu.make_async_copy(spread_ref.at[r], orthonormal_ref.at[:, r, :], sem.at[1, r]))
    for copy in copies:
        copy.start()
    for copy in copies:
        copy.wait()


def shards(ns, nm, block_input, drum_mask, panel):
    ny = ROWS_Y if ns % ROWS_Y == 0 else 2
    nz = ns // ny
    mb, rows, cols = block_input.shape
    wide = cols // nm
    n = nm * mb
    f32 = jnp.float32
    vmem = pl.BlockSpec(memory_space=pltpu.VMEM)
    hbm = pl.BlockSpec(memory_space=pl.ANY)
    dma = pltpu.SemaphoreType.DMA
    filt, spread = pl.pallas_call(
        functools.partial(whole_kernel, nz, ny, nm, float(ns * rows * cols)),
        out_shape=(
            jax.ShapeDtypeStruct((rows, mb, cols), f32),
            jax.ShapeDtypeStruct((rows, mb, cols), f32),
        ),
        in_specs=[hbm, hbm, hbm],
        out_specs=(hbm, vmem),
        scratch_shapes=[
            pltpu.VMEM((rows, mb, cols), f32),
            pltpu.VMEM((2, rows, mb, cols), f32),
            pltpu.VMEM((rows, cols), jnp.int32),
            pltpu.VMEM((2, rows, cols), jnp.int32),
            pltpu.VMEM((rows, mb, cols), f32),
            *[pltpu.VMEM((3 * rows, mb, cols + PAD), f32)] * (DEGREE + 1),
            pltpu.VMEM((3 * rows, mb, cols + PAD), f32),
            pltpu.VMEM((rows, 2 * n, wide), f32),
            pltpu.VMEM((rows, 4 * n, wide), jnp.bfloat16),
            pltpu.VMEM((2, nm, mb, 2 * n), f32),
            pltpu.VMEM((2, nm, mb, 2 * n), f32),
            pltpu.VMEM((2, mb, 2 * n), f32),
            pltpu.VMEM((2, ny, mb, 2 * n), f32),
            pltpu.VMEM((2, mb, 2 * n), f32),
            pltpu.VMEM((2, nz, mb, 2 * n), f32),
            pltpu.VMEM((2, mb, 2 * n), f32),
            pltpu.VMEM((2, nm, mb, 2 * n), f32),
            pltpu.VMEM((rows, n, wide), f32),
            dma((2 * rows + 1,)),
            dma((2, rows)), dma((2, rows)),
            dma((2,)), dma((2,)),
            dma((2,)), dma((2,)),
            dma((nm,)), dma((nm,)),
            dma((rows, nm)), dma((rows, nm)),
            dma((2, nm)), dma((2, nm)),
            dma((2, ny)), dma((2, ny)),
            dma((2, nz)), dma((2, nz)),
            dma((2, nm)), dma((2, nm)),
            dma((rows, nm)), dma((rows, nm)),
            dma((rows,)),
        ],
        compiler_params=pltpu.CompilerParams(
            collective_id=0, has_side_effects=True, vmem_limit_bytes=VMEM_LIMIT
        ),
        name="whole",
    )(block_input, drum_mask, panel)
    shape = jax.ShapeDtypeStruct((mb, rows, cols), f32)
    return pl.pallas_call(
        place_kernel,
        out_shape=(shape, shape),
        in_specs=[vmem, vmem],
        out_specs=(hbm, hbm),
        scratch_shapes=[dma((2, rows))],
        compiler_params=pltpu.CompilerParams(vmem_limit_bytes=8 << 20),
        name="place",
    )(filt, spread)


def solution(mesh):
    placed = (P("mode", "slab", None), P("slab", None), P("mode", "slab", None))
    return jax.shard_map(
        functools.partial(shards, mesh.shape["slab"], mesh.shape["mode"]),
        mesh=mesh,
        in_specs=placed,
        out_specs=(P("mode", "slab", None), P("mode", "slab", None)),
        check_vma=False,
    )
```

```python
import functools

import jax
import jax.numpy as jnp
from jax import lax
from jax.experimental import pallas as pl
from jax.experimental.pallas import tpu as pltpu
from jax.sharding import PartitionSpec as P

DEGREE = 8
ROWS_Y = 8
PAD = 128
VMEM_LIMIT = 54000 << 10

center_point = 5.0
half_width = 3.0
floor_estimate = 0.0


def filter_coefficients():
    sigma_first = half_width / (floor_estimate - center_point)
    result = [(sigma_first / half_width, 0.0)]
    sigma_now = sigma_first
    for step in range(DEGREE - 1):
        sigma_next = 1.0 / (2.0 / sigma_first - sigma_now)
        result.append((2.0 * sigma_next / half_width, sigma_now * sigma_next))
        sigma_now = sigma_next
    return result


def at(slab, mode):
    return {"slab": slab, "mode": mode}


def remote(src, dst, send, recv, where):
    return pltpu.make_async_remote_copy(
        src_ref=src,
        dst_ref=dst,
        send_sem=send,
        recv_sem=recv,
        device_id=where,
        device_id_type=pl.DeviceIdType.MESH,
    )


def exchange(src, dst, send, recv, count, me, place):
    copies = []
    for j in range(1, count):
        peer = lax.rem(me + j, count)
        copy = remote(
            src(peer), dst(me), send.at[peer], recv.at[me], place(peer)
        )
        copy.start()
        copies.append(copy)
    return copies


def arrive(src, dst, send, recv, count, me, place):
    for j in range(1, count):
        peer = lax.rem(me + j, count)
        remote(src(peer), dst(peer), send.at[peer], recv.at[peer], place(peer)).wait_recv()


def halves(value):
    high = value.astype(jnp.bfloat16)
    return high, (value - high.astype(jnp.float32)).astype(jnp.bfloat16)


def whole_kernel(
    nz, ny, nm, cells, block_ref, mask_ref, panel_ref,
    filt_ref, spread_ref,
    raw, halo, mraw, mhalo, pt, y0, y1, y2, y3, y4, y5, y6, y7, y8, mf, x, xs, part, rs, tmp, yb, tmpz, zb, tmpg, g, mixed,
    loc_sem, halo_s, halo_r, mask_s, mask_r, pass_s, pass_r, p_s, p_r, z_s, z_r, rs_s, rs_r, y_s, y_r, zz_s, zz_r, ag_s, ag_r,
    back_s, back_r, out_sem,
):
    ns = nz * ny
    slab = lax.axis_index("slab")
    m = lax.axis_index("mode")
    zi = slab // ny
    yi = lax.rem(slab, ny)
    mb, rows, cols = block_ref.shape
    wide = cols // nm
    n = nm * mb
    up = lax.rem(slab + ns - 1, ns)
    down = lax.rem(slab + 1, ns)
    y = [y0, y1, y2, y3, y4, y5, y6, y7, y8]
    pairs = filter_coefficients()
    scale = [1.0]
    for first, _ in pairs:
        scale.append(-first * scale[-1])
    drag = [0.0, 0.0] + [pairs[k - 1][1] * scale[k - 2] / scale[k] for k in range(2, DEGREE + 1)]
    last = DEGREE

    local = [pltpu.make_async_copy(mask_ref, mraw, loc_sem.at[2 * rows])]
    local += [pltpu.make_async_copy(block_ref.at[:, r, :], raw.at[r], loc_sem.at[r]) for r in range(rows)]
    late = [pltpu.make_async_copy(panel_ref.at[:, r, :], pt.at[r], loc_sem.at[rows + r]) for r in range(rows)]
    for copy in local:
        copy.start()

    barrier = pltpu.get_barrier_semaphore()

    def greet(where):
        pl.semaphore_signal(barrier, inc=1, device_id=where, device_id_type=pl.DeviceIdType.MESH)

    greet(at(up, m))
    greet(at(down, m))
    for j in range(1, nm):
        greet(at(slab, lax.rem(m + j, nm)))
    for j in range(1, ny):
        greet(at(zi * ny + lax.rem(yi + j, ny), m))
    for j in range(1, nz):
        greet(at(lax.rem(zi + j, nz) * ny + yi, m))
    local[0].wait()
    pl.semaphore_wait(barrier, 2 + nm - 1 + ny - 1 + nz - 1)

    sends = []
    core = lax.rem(m, 2)
    other = m + 1 - 2 * core
    half = pl.ds(pl.multiple_of(core * (cols // 2), 128), cols // 2)
    rest = pl.ds(pl.multiple_of((1 - core) * (cols // 2), 128), cols // 2)
    mask_copies = [
        remote(mraw.at[:, half], mhalo.at[0, :, half], mask_s.at[0], mask_r.at[0], at(down, m)),
        remote(mraw.at[:, half], mhalo.at[1, :, half], mask_s.at[1], mask_r.at[1], at(up, m)),
    ]
    mask_passes = [
        remote(mhalo.at[side, :, half], mhalo.at[side, :, half], pass_s.at[side], pass_r.at[side], at(slab, other))
        for side in range(2)
    ]
    mask_lands = [
        remote(mhalo.at[side, :, rest], mhalo.at[side, :, rest], pass_s.at[side], pass_r.at[side], at(slab, other))
        for side in range(2)
    ]
    for copy in mask_copies:
        copy.start()
    halo_copies = [[], []]
    for d in range(1, rows + 1):
        lo, hi = rows - d, d - 1
        if lo > hi:
            local[1 + lo].wait()
            local[1 + hi].wait()
        top = remote(raw.at[lo], halo.at[0, lo], halo_s.at[0, lo], halo_r.at[0, lo], at(down, m))
        bottom = remote(raw.at[hi], halo.at[1, hi], halo_s.at[1, hi], halo_r.at[1, hi], at(up, m))
        top.start()
        bottom.start()
        halo_copies[0].append(top)
        halo_copies[1].append(bottom)
    for copy in late:
        copy.start()
    for copy in late:
        copy.wait()

    def mates(peer):
        return at(slab, peer)

    def along_y(peer):
        return at(zi * ny + peer, m)

    def along_z(peer):
        return at(peer * ny + yi, m)

    def columns(peer):
        return pl.ds(pl.multiple_of(peer * wide, wide), wide)

    def eight(peer, base=0):
        return pl.ds(pl.multiple_of(base + peer * mb, mb), mb)

    p_src = lambda peer: pt.at[:, :, columns(peer)]
    p_dst = lambda who: x.at[:, eight(who, n), :]
    sends += exchange(p_src, p_dst, p_s, p_r, nm, m, mates)
    x[:, eight(m, n), :] = pt[:, :, columns(m)]

    zero_pad = jnp.zeros((mb, PAD), jnp.float32)
    for r in range(rows):
        row = jnp.broadcast_to(mraw[r:r + 1, :].astype(jnp.float32), (mb, cols))
        mf[rows + r, :, :cols] = row
        mf[rows + r, :, cols:] = zero_pad
        y0[rows + r, :, :cols] = raw[r] * row
        y0[rows + r, :, cols:] = zero_pad

    def row_step(k, r):
        here = y[k - 1][r]
        total = here + y[k - 1][r - 1] + y[k - 1][r + 1]
        total = total + pltpu.roll(here, 1, 1) + pltpu.roll(here, cols + PAD - 1, 1)
        new = mf[r] * total
        if k > 1:
            new = new - y[k - 2][r] * drag[k]
        y[k][r] = new * scale[k] if k == last else new

    def stage(d):
        for k in range(1, min(last, d + 3) + 1):
            row_step(k, rows - d + k)
            row_step(k, 2 * rows - 1 + d - k)

    for k in range(1, rows // 2):
        for r in range(rows + k, 2 * rows - k):
            row_step(k, r)

    for side in range(2):
        mask_copies[side].wait_recv()
        mask_passes[side].start()
    for copy in mask_lands:
        copy.wait_recv()
    inside = [jnp.where(slab > 0, 1.0, 0.0), jnp.where(slab < ns - 1, 1.0, 0.0)]
    for side in range(2):
        for r in range(rows):
            index = r if side == 0 else 2 * rows + r
            row = mhalo[side, r:r + 1, :].astype(jnp.float32) * inside[side]
            mf[index, :, :cols] = jnp.broadcast_to(row, (mb, cols))
            mf[index, :, cols:] = zero_pad

    z_src = lambda r: (lambda peer: y8.at[rows + r, :, columns(peer)])
    z_dst = lambda r: (lambda who: x.at[r, eight(who), :])
    contract = (((1,), (1,)), ((), ()))

    def products(left, right):
        return lax.dot_general(left, right, contract, preferred_element_type=jnp.float32)

    def panel_gram(r):
        high, low = halves(x[r, n:, :])
        xs[r, n:2 * n, :] = high
        xs[r, 3 * n:, :] = low
        mixed_part = products(high, low)
        return products(high, high) + products(low, low), mixed_part

    def block_gram(r):
        arrive(z_src(r), z_dst(r), z_s.at[r], z_r.at[r], nm, m, mates)
        high, low = halves(x[r, :n, :])
        xs[r, :n, :] = high
        xs[r, 2 * n:3 * n, :] = low
        all_high, all_low = xs[r, :2 * n, :], xs[r, 2 * n:, :]
        return (
            products(high, all_high) + products(low, all_low) + products(high, all_low) + products(low, all_high)
        )

    def reduce_out(which):
        rs[which, m] = part[which, m]
        return exchange(
            lambda peer: part.at[which, peer], lambda who: rs.at[which, who],
            rs_s.at[which], rs_r.at[which], nm, m, mates,
        )

    panel_part = jnp.zeros((n, n), jnp.float32)
    panel_mixed = jnp.zeros((n, n), jnp.float32)
    block_part = jnp.zeros((n, 2 * n), jnp.float32)
    quarter = rows // 4
    panel_rows = {
        rows - 3: list(range(quarter, rows - quarter)),
        rows - 2: list(range(quarter)) + list(range(rows - quarter, rows)),
    }
    outs = []
    for d in range(1, rows + 1):
        for side, r in ((0, rows - d), (1, d - 1)):
            halo_copies[side][d - 1].wait_recv()
            index = r if side == 0 else 2 * rows + r
            y0[index, :, :cols] = halo[side, r] * mf[index, :, :cols]
            y0[index, :, cols:] = zero_pad
        stage(d)
        if d > rows // 2:
            for r in (rows - d, d - 1):
                sends += exchange(z_src(r), z_dst(r), z_s.at[r], z_r.at[r], nm, m, mates)
                x[r, eight(m), :] = y8[rows + r, :, columns(m)]
                out = pltpu.make_async_copy(y8.at[rows + r, :, pl.ds(0, cols)], filt_ref.at[r], out_sem.at[r])
                out.start()
                outs.append(out)
        if d in panel_rows:
            if d == rows - 3:
                arrive(p_src, p_dst, p_s, p_r, nm, m, mates)
            for r in panel_rows[d]:
                same, cross = panel_gram(r)
                panel_part += same
                panel_mixed += cross
        if d == rows - 2:
            panel_all = panel_part + panel_mixed + panel_mixed.T
            panel_all = jnp.concatenate([panel_all, jnp.zeros((n, n), jnp.float32)], axis=1)
            for j in range(nm):
                part[1, j] = panel_all[j * mb:(j + 1) * mb]
            sends += reduce_out(1)
        if d > rows // 2 + 1:
            for r in (rows - d + 1, d - 2):
                block_part += block_gram(r)

    def sum_and_send(which, from_buf, from_s, from_r, count, me, place, out, to_buf, to_s, to_r, to_count, to_me, to_place):
        arrive(lambda peer: out.at[which], lambda who: from_buf.at[which, who], from_s.at[which], from_r.at[which], count, me, place)
        total = from_buf[which, 0]
        for j in range(1, count):
            total = total + from_buf[which, j]
        out[which] = total
        to_buf[which, to_me] = total
        return exchange(
            lambda peer: out.at[which], lambda who: to_buf.at[which, who],
            to_s.at[which], to_r.at[which], to_count, to_me, to_place,
        )

    def to_y(which):
        return sum_and_send(which, rs, rs_s, rs_r, nm, m, mates, tmp, yb, y_s, y_r, ny, yi, along_y)

    def to_z(which):
        return sum_and_send(which, yb, y_s, y_r, ny, yi, along_y, tmpz, zb, zz_s, zz_r, nz, zi, along_z)

    def to_all(which):
        return sum_and_send(which, zb, zz_s, zz_r, nz, zi, along_z, tmpg, g, ag_s, ag_r, nm, m, mates)

    def finish(which):
        arrive(lambda peer: tmpg.at[which], lambda who: g.at[which, who], ag_s.at[which], ag_r.at[which], nm, m, mates)

    for r in (0, rows - 1):
        block_part += block_gram(r)
    for j in range(nm):
        part[0, j] = block_part[j * mb:(j + 1) * mb]
    sends += reduce_out(0)
    sends += to_y(1)
    sends += to_y(0)
    sends += to_z(1)
    sends += to_z(0)
    sends += to_all(1)
    sends += to_all(0)
    finish(1)
    finish(0)

    top = g[0].reshape(n, 2 * n)
    panel = g[1].reshape(n, 2 * n)
    full = jnp.concatenate(
        [top, jnp.concatenate([top[:, n:].T, panel[:, :n]], axis=1)], axis=0
    )
    w_high, w_low = halves(eliminate(full, n, mb, 2 * n // mb, cells))
    back_src = lambda r: (lambda peer: mixed.at[r, eight(peer), :])
    back_dst = lambda r: (lambda who: spread_ref.at[r, :, columns(who)])
    for r in range(rows):
        high, low = xs[r, :2 * n, :], xs[r, 2 * n:, :]
        mixed[r] = (
            jnp.dot(w_high, high, preferred_element_type=jnp.float32)
            + jnp.dot(w_high, low, preferred_element_type=jnp.float32)
            + jnp.dot(w_low, high, preferred_element_type=jnp.float32)
        )
        sends += exchange(back_src(r), back_dst(r), back_s.at[r], back_r.at[r], nm, m, mates)
        spread_ref[r, :, columns(m)] = mixed[r, eight(m), :]
    for r in range(rows):
        arrive(back_src(r), back_dst(r), back_s.at[r], back_r.at[r], nm, m, mates)

    for copy in outs:
        copy.wait()
    for copy in sends + mask_copies + mask_passes + halo_copies[0] + halo_copies[1]:
        copy.wait_send()


def eliminate(full, n, mb, nb, cells):
    width = 2 * n
    a = [full[i * mb:(i + 1) * mb] for i in range(nb)]
    lane = lax.broadcasted_iota(jnp.int32, (mb, width), 1)
    sub = lax.broadcasted_iota(jnp.int32, (mb, width), 0)
    result = []
    for b in range(nb):
        base = b * mb
        inside = (lane >= base) & (lane < base + mb)
        block = a[b]
        rowb = [jnp.broadcast_to(block[i:i + 1, :], (mb, width)) for i in range(mb)]
        own = [jnp.broadcast_to(block[:, base + k:base + k + 1], (mb, width)) for k in range(mb)]
        e = [[jnp.broadcast_to(own[j][i:i + 1, :], (mb, width)) for j in range(i + 1)] for i in range(mb)]
        later = range(b + 1, nb)
        column = {
            i: [jnp.broadcast_to(a[i][:, base + k:base + k + 1], (mb, width)) for k in range(mb)] for i in later
        }
        row = [jnp.where(inside, jnp.where(lane == base + i, 1.0, 0.0), rowb[i]) for i in range(mb)]
        pivot, inverse = [], []
        f = [[None] * mb for _ in range(mb)]
        for k in range(0, mb, 2):
            first, link = e[k][k], e[k + 1][k]
            det = first * e[k + 1][k + 1] - link * link
            first_inverse = 1.0 / first
            pivot += [first, det * first_inverse]
            inverse += [first_inverse, first * (1.0 / det)]
            for step in (k, k + 1):
                for i in range(step + 1, mb):
                    f[i][step] = e[i][step] * inverse[step]
                for i in range(step + 1, mb):
                    for j in range(step + 1, i + 1):
                        e[i][j] = e[i][j] - f[i][step] * e[j][step]
                    row[i] = row[i] - f[i][step] * row[step]
        if base >= n:
            scaled = jnp.zeros((mb, width), jnp.float32)
            for i in range(mb):
                scaled = jnp.where(sub == i, row[i] * lax.rsqrt(pivot[i] * (1.0 / cells)), scaled)
            result.append(jnp.where(lane < base + mb, scaled, 0.0))
        if b == nb - 1:
            break
        v = [row[i] * inverse[i] for i in range(mb)]
        for k in reversed(range(mb)):
            for i in range(k):
                v[i] = v[i] - f[k][i] * v[k]
        for i in later:
            total = column[i][0] * v[0]
            for k in range(1, mb):
                total = total + column[i][k] * v[k]
            a[i] = jnp.where(inside, 0.0, a[i]) - total
    return jnp.concatenate(result, axis=0)


def place_kernel(filt_ref, spread_ref, filtered_ref, orthonormal_ref, sem):
    copies = []
    for r in range(filt_ref.shape[0]):
        copies.append(pltpu.make_async_copy(filt_ref.at[r], filtered_ref.at[:, r, :], sem.at[0, r]))
        copies.append(pltpu.make_async_copy(spread_ref.at[r], orthonormal_ref.at[:, r, :], sem.at[1, r]))
    for copy in copies:
        copy.start()
    for copy in copies:
        copy.wait()


def shards(ns, nm, block_input, drum_mask, panel):
    ny = ROWS_Y if ns % ROWS_Y == 0 else 2
    nz = ns // ny
    mb, rows, cols = block_input.shape
    wide = cols // nm
    n = nm * mb
    f32 = jnp.float32
    vmem = pl.BlockSpec(memory_space=pltpu.VMEM)
    hbm = pl.BlockSpec(memory_space=pl.ANY)
    dma = pltpu.SemaphoreType.DMA
    filt, spread = pl.pallas_call(
        functools.partial(whole_kernel, nz, ny, nm, float(ns * rows * cols)),
        out_shape=(
            jax.ShapeDtypeStruct((rows, mb, cols), f32),
            jax.ShapeDtypeStruct((rows, mb, cols), f32),
        ),
        in_specs=[hbm, hbm, hbm],
        out_specs=(hbm, vmem),
        scratch_shapes=[
            pltpu.VMEM((rows, mb, cols), f32),
            pltpu.VMEM((2, rows, mb, cols), f32),
            pltpu.VMEM((rows, cols), jnp.int32),
            pltpu.VMEM((2, rows, cols), jnp.int32),
            pltpu.VMEM((rows, mb, cols), f32),
            *[pltpu.VMEM((3 * rows, mb, cols + PAD), f32)] * (DEGREE + 1),
            pltpu.VMEM((3 * rows, mb, cols + PAD), f32),
            pltpu.VMEM((rows, 2 * n, wide), f32),
            pltpu.VMEM((rows, 4 * n, wide), jnp.bfloat16),
            pltpu.VMEM((2, nm, mb, 2 * n), f32),
            pltpu.VMEM((2, nm, mb, 2 * n), f32),
            pltpu.VMEM((2, mb, 2 * n), f32),
            pltpu.VMEM((2, ny, mb, 2 * n), f32),
            pltpu.VMEM((2, mb, 2 * n), f32),
            pltpu.VMEM((2, nz, mb, 2 * n), f32),
            pltpu.VMEM((2, mb, 2 * n), f32),
            pltpu.VMEM((2, nm, mb, 2 * n), f32),
            pltpu.VMEM((rows, n, wide), f32),
            dma((2 * rows + 1,)),
            dma((2, rows)), dma((2, rows)),
            dma((2,)), dma((2,)),
            dma((2,)), dma((2,)),
            dma((nm,)), dma((nm,)),
            dma((rows, nm)), dma((rows, nm)),
            dma((2, nm)), dma((2, nm)),
            dma((2, ny)), dma((2, ny)),
            dma((2, nz)), dma((2, nz)),
            dma((2, nm)), dma((2, nm)),
            dma((rows, nm)), dma((rows, nm)),
            dma((rows,)),
        ],
        compiler_params=pltpu.CompilerParams(
            collective_id=0, has_side_effects=True, vmem_limit_bytes=VMEM_LIMIT
        ),
        name="whole",
    )(block_input, drum_mask, panel)
    shape = jax.ShapeDtypeStruct((mb, rows, cols), f32)
    return pl.pallas_call(
        place_kernel,
        out_shape=(shape, shape),
        in_specs=[vmem, vmem],
        out_specs=(hbm, hbm),
        scratch_shapes=[dma((2, rows))],
        compiler_params=pltpu.CompilerParams(vmem_limit_bytes=8 << 20),
        name="place",
    )(filt, spread)


def solution(mesh):
    placed = (P("mode", "slab", None), P("slab", None), P("mode", "slab", None))
    return jax.shard_map(
        functools.partial(shards, mesh.shape["slab"], mesh.shape["mode"]),
        mesh=mesh,
        in_specs=placed,
        out_specs=(P("mode", "slab", None), P("mode", "slab", None)),
        check_vma=False,
    )
```

```python
import functools

import jax
import jax.numpy as jnp
from jax import lax
from jax.experimental import pallas as pl
from jax.experimental.pallas import tpu as pltpu
from jax.sharding import PartitionSpec as P

DEGREE = 8
ROWS_Y = 8
PAD = 128
VMEM_LIMIT = 54000 << 10

center_point = 5.0
half_width = 3.0
floor_estimate = 0.0


def filter_coefficients():
    sigma_first = half_width / (floor_estimate - center_point)
    result = [(sigma_first / half_width, 0.0)]
    sigma_now = sigma_first
    for step in range(DEGREE - 1):
        sigma_next = 1.0 / (2.0 / sigma_first - sigma_now)
        result.append((2.0 * sigma_next / half_width, sigma_now * sigma_next))
        sigma_now = sigma_next
    return result


def at(slab, mode):
    return {"slab": slab, "mode": mode}


def remote(src, dst, send, recv, where):
    return pltpu.make_async_remote_copy(
        src_ref=src,
        dst_ref=dst,
        send_sem=send,
        recv_sem=recv,
        device_id=where,
        device_id_type=pl.DeviceIdType.MESH,
    )


def exchange(src, dst, send, recv, count, me, place):
    copies = []
    for j in range(1, count):
        peer = lax.rem(me + j, count)
        copy = remote(
            src(peer), dst(me), send.at[peer], recv.at[me], place(peer)
        )
        copy.start()
        copies.append(copy)
    return copies


def arrive(src, dst, send, recv, count, me, place):
    for j in range(1, count):
        peer = lax.rem(me + j, count)
        remote(src(peer), dst(peer), send.at[peer], recv.at[peer], place(peer)).wait_recv()


def halves(value):
    high = value.astype(jnp.bfloat16)
    return high, (value - high.astype(jnp.float32)).astype(jnp.bfloat16)


def whole_kernel(
    nz, ny, nm, cells, block_ref, mask_ref, panel_ref,
    filt_ref, spread_ref,
    raw, halo, mraw, mhalo, pt, y0, y1, y2, y3, y4, y5, y6, y7, y8, mf, x, xs, part, rs, tmp, yb, tmpz, zb, tmpg, g, mixed,
    loc_sem, halo_s, halo_r, mask_s, mask_r, pass_s, pass_r, p_s, p_r, z_s, z_r, rs_s, rs_r, y_s, y_r, zz_s, zz_r, ag_s, ag_r,
    back_s, back_r, out_sem, known,
):
    ns = nz * ny
    slab = lax.axis_index("slab")
    m = lax.axis_index("mode")
    zi = slab // ny
    yi = lax.rem(slab, ny)
    mb, rows, cols = block_ref.shape
    wide = cols // nm
    n = nm * mb
    up = lax.rem(slab + ns - 1, ns)
    down = lax.rem(slab + 1, ns)
    y = [y0, y1, y2, y3, y4, y5, y6, y7, y8]
    pairs = filter_coefficients()
    scale = [1.0]
    for first, _ in pairs:
        scale.append(-first * scale[-1])
    drag = [0.0, 0.0] + [pairs[k - 1][1] * scale[k - 2] / scale[k] for k in range(2, DEGREE + 1)]
    last = DEGREE

    local = [pltpu.make_async_copy(mask_ref, mraw, loc_sem.at[2 * rows])]
    local += [pltpu.make_async_copy(block_ref.at[:, r, :], raw.at[r], loc_sem.at[r]) for r in range(rows)]
    late = [pltpu.make_async_copy(panel_ref.at[:, r, :], pt.at[r], loc_sem.at[rows + r]) for r in range(rows)]
    for copy in local:
        copy.start()

    barrier = pltpu.get_barrier_semaphore()

    def greet(where):
        pl.semaphore_signal(barrier, inc=1, device_id=where, device_id_type=pl.DeviceIdType.MESH)

    greet(at(up, m))
    greet(at(down, m))
    for j in range(1, nm):
        greet(at(slab, lax.rem(m + j, nm)))
    def near(step):
        return [
            at(zi * ny + lax.rem(yi + step, ny), m),
            at(zi * ny + lax.rem(yi + ny - step, ny), m),
            at(lax.rem(zi + step, nz) * ny + yi, m),
            at(lax.rem(zi + nz - step, nz) * ny + yi, m),
        ]

    def tell(index, step):
        for where in near(step):
            pl.semaphore_signal(
                known.at[index], inc=1, device_id=where, device_id_type=pl.DeviceIdType.MESH
            )

    for where in near(1):
        greet(where)
    local[0].wait()
    pl.semaphore_wait(barrier, 2 + nm - 1 + 4)

    sends = []
    core = lax.rem(m, 2)
    other = m + 1 - 2 * core
    half = pl.ds(pl.multiple_of(core * (cols // 2), 128), cols // 2)
    rest = pl.ds(pl.multiple_of((1 - core) * (cols // 2), 128), cols // 2)
    mask_copies = [
        remote(mraw.at[:, half], mhalo.at[0, :, half], mask_s.at[0], mask_r.at[0], at(down, m)),
        remote(mraw.at[:, half], mhalo.at[1, :, half], mask_s.at[1], mask_r.at[1], at(up, m)),
    ]
    mask_passes = [
        remote(mhalo.at[side, :, half], mhalo.at[side, :, half], pass_s.at[side], pass_r.at[side], at(slab, other))
        for side in range(2)
    ]
    mask_lands = [
        remote(mhalo.at[side, :, rest], mhalo.at[side, :, rest], pass_s.at[side], pass_r.at[side], at(slab, other))
        for side in range(2)
    ]
    for copy in mask_copies:
        copy.start()
    halo_copies = [[], []]
    for d in range(1, rows + 1):
        lo, hi = rows - d, d - 1
        if lo > hi:
            local[1 + lo].wait()
            local[1 + hi].wait()
        top = remote(raw.at[lo], halo.at[0, lo], halo_s.at[0, lo], halo_r.at[0, lo], at(down, m))
        bottom = remote(raw.at[hi], halo.at[1, hi], halo_s.at[1, hi], halo_r.at[1, hi], at(up, m))
        top.start()
        bottom.start()
        halo_copies[0].append(top)
        halo_copies[1].append(bottom)
    for copy in late:
        copy.start()
    tell(0, 1)
    for copy in late:
        copy.wait()

    def mates(peer):
        return at(slab, peer)

    def along_y(peer):
        return at(zi * ny + peer, m)

    def along_z(peer):
        return at(peer * ny + yi, m)

    def columns(peer):
        return pl.ds(pl.multiple_of(peer * wide, wide), wide)

    def eight(peer, base=0):
        return pl.ds(pl.multiple_of(base + peer * mb, mb), mb)

    p_src = lambda peer: pt.at[:, :, columns(peer)]
    p_dst = lambda who: x.at[:, eight(who, n), :]
    sends += exchange(p_src, p_dst, p_s, p_r, nm, m, mates)
    x[:, eight(m, n), :] = pt[:, :, columns(m)]

    zero_pad = jnp.zeros((mb, PAD), jnp.float32)
    for r in range(rows):
        row = jnp.broadcast_to(mraw[r:r + 1, :].astype(jnp.float32), (mb, cols))
        mf[rows + r, :, :cols] = row
        mf[rows + r, :, cols:] = zero_pad
        y0[rows + r, :, :cols] = raw[r] * row
        y0[rows + r, :, cols:] = zero_pad

    def row_step(k, r):
        here = y[k - 1][r]
        total = here + y[k - 1][r - 1] + y[k - 1][r + 1]
        total = total + pltpu.roll(here, 1, 1) + pltpu.roll(here, cols + PAD - 1, 1)
        new = mf[r] * total
        if k > 1:
            new = new - y[k - 2][r] * drag[k]
        y[k][r] = new * scale[k] if k == last else new

    def stage(d):
        for k in range(1, min(last, d + 3) + 1):
            row_step(k, rows - d + k)
            row_step(k, 2 * rows - 1 + d - k)

    for k in range(1, rows // 2):
        for r in range(rows + k, 2 * rows - k):
            row_step(k, r)

    pl.semaphore_wait(known.at[0], 4)
    tell(1, 2)
    for side in range(2):
        mask_copies[side].wait_recv()
        mask_passes[side].start()
    for copy in mask_lands:
        copy.wait_recv()
    inside = [jnp.where(slab > 0, 1.0, 0.0), jnp.where(slab < ns - 1, 1.0, 0.0)]
    for side in range(2):
        for r in range(rows):
            index = r if side == 0 else 2 * rows + r
            row = mhalo[side, r:r + 1, :].astype(jnp.float32) * inside[side]
            mf[index, :, :cols] = jnp.broadcast_to(row, (mb, cols))
            mf[index, :, cols:] = zero_pad

    z_src = lambda r: (lambda peer: y8.at[rows + r, :, columns(peer)])
    z_dst = lambda r: (lambda who: x.at[r, eight(who), :])
    contract = (((1,), (1,)), ((), ()))

    def products(left, right):
        return lax.dot_general(left, right, contract, preferred_element_type=jnp.float32)

    def panel_gram(r):
        high, low = halves(x[r, n:, :])
        xs[r, n:2 * n, :] = high
        xs[r, 3 * n:, :] = low
        mixed_part = products(high, low)
        return products(high, high) + products(low, low), mixed_part

    def block_gram(r):
        arrive(z_src(r), z_dst(r), z_s.at[r], z_r.at[r], nm, m, mates)
        high, low = halves(x[r, :n, :])
        xs[r, :n, :] = high
        xs[r, 2 * n:3 * n, :] = low
        all_high, all_low = xs[r, :2 * n, :], xs[r, 2 * n:, :]
        return (
            products(high, all_high) + products(low, all_low) + products(high, all_low) + products(low, all_high)
        )

    def reduce_out(which):
        rs[which, m] = part[which, m]
        return exchange(
            lambda peer: part.at[which, peer], lambda who: rs.at[which, who],
            rs_s.at[which], rs_r.at[which], nm, m, mates,
        )

    panel_part = jnp.zeros((n, n), jnp.float32)
    panel_mixed = jnp.zeros((n, n), jnp.float32)
    block_part = jnp.zeros((n, 2 * n), jnp.float32)
    quarter = rows // 4
    panel_rows = {
        rows - 3: list(range(quarter, rows - quarter)),
        rows - 2: list(range(quarter)) + list(range(rows - quarter, rows)),
    }
    outs = []
    for d in range(1, rows + 1):
        for side, r in ((0, rows - d), (1, d - 1)):
            halo_copies[side][d - 1].wait_recv()
            index = r if side == 0 else 2 * rows + r
            y0[index, :, :cols] = halo[side, r] * mf[index, :, :cols]
            y0[index, :, cols:] = zero_pad
        stage(d)
        if d > rows // 2:
            for r in (rows - d, d - 1):
                sends += exchange(z_src(r), z_dst(r), z_s.at[r], z_r.at[r], nm, m, mates)
                x[r, eight(m), :] = y8[rows + r, :, columns(m)]
                out = pltpu.make_async_copy(y8.at[rows + r, :, pl.ds(0, cols)], filt_ref.at[r], out_sem.at[r])
                out.start()
                outs.append(out)
        if d in panel_rows:
            if d == rows - 3:
                arrive(p_src, p_dst, p_s, p_r, nm, m, mates)
            for r in panel_rows[d]:
                same, cross = panel_gram(r)
                panel_part += same
                panel_mixed += cross
        if d == rows - 2:
            pl.semaphore_wait(known.at[1], 4)
            panel_all = panel_part + panel_mixed + panel_mixed.T
            panel_all = jnp.concatenate([panel_all, jnp.zeros((n, n), jnp.float32)], axis=1)
            for j in range(nm):
                part[1, j] = panel_all[j * mb:(j + 1) * mb]
            sends += reduce_out(1)
        if d > rows // 2 + 1:
            for r in (rows - d + 1, d - 2):
                block_part += block_gram(r)

    def sum_and_send(which, from_buf, from_s, from_r, count, me, place, out, to_buf, to_s, to_r, to_count, to_me, to_place):
        arrive(lambda peer: out.at[which], lambda who: from_buf.at[which, who], from_s.at[which], from_r.at[which], count, me, place)
        total = from_buf[which, 0]
        for j in range(1, count):
            total = total + from_buf[which, j]
        out[which] = total
        to_buf[which, to_me] = total
        return exchange(
            lambda peer: out.at[which], lambda who: to_buf.at[which, who],
            to_s.at[which], to_r.at[which], to_count, to_me, to_place,
        )

    def to_y(which):
        return sum_and_send(which, rs, rs_s, rs_r, nm, m, mates, tmp, yb, y_s, y_r, ny, yi, along_y)

    def to_z(which):
        return sum_and_send(which, yb, y_s, y_r, ny, yi, along_y, tmpz, zb, zz_s, zz_r, nz, zi, along_z)

    def to_all(which):
        return sum_and_send(which, zb, zz_s, zz_r, nz, zi, along_z, tmpg, g, ag_s, ag_r, nm, m, mates)

    def finish(which):
        arrive(lambda peer: tmpg.at[which], lambda who: g.at[which, who], ag_s.at[which], ag_r.at[which], nm, m, mates)

    for r in (0, rows - 1):
        block_part += block_gram(r)
    for j in range(nm):
        part[0, j] = block_part[j * mb:(j + 1) * mb]
    sends += reduce_out(0)
    sends += to_y(1)
    sends += to_y(0)
    sends += to_z(1)
    sends += to_z(0)
    sends += to_all(1)
    sends += to_all(0)
    finish(1)
    finish(0)

    top = g[0].reshape(n, 2 * n)
    panel = g[1].reshape(n, 2 * n)
    full = jnp.concatenate(
        [top, jnp.concatenate([top[:, n:].T, panel[:, :n]], axis=1)], axis=0
    )
    w_high, w_low = halves(eliminate(full, n, mb, 2 * n // mb, cells))
    back_src = lambda r: (lambda peer: mixed.at[r, eight(peer), :])
    back_dst = lambda r: (lambda who: spread_ref.at[r, :, columns(who)])
    for r in range(rows):
        high, low = xs[r, :2 * n, :], xs[r, 2 * n:, :]
        mixed[r] = (
            jnp.dot(w_high, high, preferred_element_type=jnp.float32)
            + jnp.dot(w_high, low, preferred_element_type=jnp.float32)
            + jnp.dot(w_low, high, preferred_element_type=jnp.float32)
        )
        sends += exchange(back_src(r), back_dst(r), back_s.at[r], back_r.at[r], nm, m, mates)
        spread_ref[r, :, columns(m)] = mixed[r, eight(m), :]
    for r in range(rows):
        arrive(back_src(r), back_dst(r), back_s.at[r], back_r.at[r], nm, m, mates)

    for copy in outs:
        copy.wait()
    for copy in sends + mask_copies + mask_passes + halo_copies[0] + halo_copies[1]:
        copy.wait_send()


def eliminate(full, n, mb, nb, cells):
    width = 2 * n
    a = [full[i * mb:(i + 1) * mb] for i in range(nb)]
    lane = lax.broadcasted_iota(jnp.int32, (mb, width), 1)
    sub = lax.broadcasted_iota(jnp.int32, (mb, width), 0)
    result = []
    for b in range(nb):
        base = b * mb
        inside = (lane >= base) & (lane < base + mb)
        block = a[b]
        rowb = [jnp.broadcast_to(block[i:i + 1, :], (mb, width)) for i in range(mb)]
        own = [jnp.broadcast_to(block[:, base + k:base + k + 1], (mb, width)) for k in range(mb)]
        e = [[jnp.broadcast_to(own[j][i:i + 1, :], (mb, width)) for j in range(i + 1)] for i in range(mb)]
        later = range(b + 1, nb)
        column = {
            i: [jnp.broadcast_to(a[i][:, base + k:base + k + 1], (mb, width)) for k in range(mb)] for i in later
        }
        row = [jnp.where(inside, jnp.where(lane == base + i, 1.0, 0.0), rowb[i]) for i in range(mb)]
        pivot, inverse = [], []
        f = [[None] * mb for _ in range(mb)]
        for k in range(0, mb, 2):
            first, link = e[k][k], e[k + 1][k]
            det = first * e[k + 1][k + 1] - link * link
            first_inverse = 1.0 / first
            pivot += [first, det * first_inverse]
            inverse += [first_inverse, first * (1.0 / det)]
            for step in (k, k + 1):
                for i in range(step + 1, mb):
                    f[i][step] = e[i][step] * inverse[step]
                for i in range(step + 1, mb):
                    for j in range(step + 1, i + 1):
                        e[i][j] = e[i][j] - f[i][step] * e[j][step]
                    row[i] = row[i] - f[i][step] * row[step]
        if base >= n:
            scaled = jnp.zeros((mb, width), jnp.float32)
            for i in range(mb):
                scaled = jnp.where(sub == i, row[i] * lax.rsqrt(pivot[i] * (1.0 / cells)), scaled)
            result.append(jnp.where(lane < base + mb, scaled, 0.0))
        if b == nb - 1:
            break
        v = [row[i] * inverse[i] for i in range(mb)]
        for k in reversed(range(mb)):
            for i in range(k):
                v[i] = v[i] - f[k][i] * v[k]
        for i in later:
            total = column[i][0] * v[0]
            for k in range(1, mb):
                total = total + column[i][k] * v[k]
            a[i] = jnp.where(inside, 0.0, a[i]) - total
    return jnp.concatenate(result, axis=0)


def place_kernel(filt_ref, spread_ref, filtered_ref, orthonormal_ref, sem):
    copies = []
    for r in range(filt_ref.shape[0]):
        copies.append(pltpu.make_async_copy(filt_ref.at[r], filtered_ref.at[:, r, :], sem.at[0, r]))
        copies.append(pltpu.make_async_copy(spread_ref.at[r], orthonormal_ref.at[:, r, :], sem.at[1, r]))
    for copy in copies:
        copy.start()
    for copy in copies:
        copy.wait()


def shards(ns, nm, block_input, drum_mask, panel):
    ny = ROWS_Y if ns % ROWS_Y == 0 else 2
    nz = ns // ny
    mb, rows, cols = block_input.shape
    wide = cols // nm
    n = nm * mb
    f32 = jnp.float32
    vmem = pl.BlockSpec(memory_space=pltpu.VMEM)
    hbm = pl.BlockSpec(memory_space=pl.ANY)
    dma = pltpu.SemaphoreType.DMA
    filt, spread = pl.pallas_call(
        functools.partial(whole_kernel, nz, ny, nm, float(ns * rows * cols)),
        out_shape=(
            jax.ShapeDtypeStruct((rows, mb, cols), f32),
            jax.ShapeDtypeStruct((rows, mb, cols), f32),
        ),
        in_specs=[hbm, hbm, hbm],
        out_specs=(hbm, vmem),
        scratch_shapes=[
            pltpu.VMEM((rows, mb, cols), f32),
            pltpu.VMEM((2, rows, mb, cols), f32),
            pltpu.VMEM((rows, cols), jnp.int32),
            pltpu.VMEM((2, rows, cols), jnp.int32),
            pltpu.VMEM((rows, mb, cols), f32),
            *[pltpu.VMEM((3 * rows, mb, cols + PAD), f32)] * (DEGREE + 1),
            pltpu.VMEM((3 * rows, mb, cols + PAD), f32),
            pltpu.VMEM((rows, 2 * n, wide), f32),
            pltpu.VMEM((rows, 4 * n, wide), jnp.bfloat16),
            pltpu.VMEM((2, nm, mb, 2 * n), f32),
            pltpu.VMEM((2, nm, mb, 2 * n), f32),
            pltpu.VMEM((2, mb, 2 * n), f32),
            pltpu.VMEM((2, ny, mb, 2 * n), f32),
            pltpu.VMEM((2, mb, 2 * n), f32),
            pltpu.VMEM((2, nz, mb, 2 * n), f32),
            pltpu.VMEM((2, mb, 2 * n), f32),
            pltpu.VMEM((2, nm, mb, 2 * n), f32),
            pltpu.VMEM((rows, n, wide), f32),
            dma((2 * rows + 1,)),
            dma((2, rows)), dma((2, rows)),
            dma((2,)), dma((2,)),
            dma((2,)), dma((2,)),
            dma((nm,)), dma((nm,)),
            dma((rows, nm)), dma((rows, nm)),
            dma((2, nm)), dma((2, nm)),
            dma((2, ny)), dma((2, ny)),
            dma((2, nz)), dma((2, nz)),
            dma((2, nm)), dma((2, nm)),
            dma((rows, nm)), dma((rows, nm)),
            dma((rows,)),
            pltpu.SemaphoreType.REGULAR((2,)),
        ],
        compiler_params=pltpu.CompilerParams(
            collective_id=0, has_side_effects=True, vmem_limit_bytes=VMEM_LIMIT
        ),
        name="whole",
    )(block_input, drum_mask, panel)
    shape = jax.ShapeDtypeStruct((mb, rows, cols), f32)
    return pl.pallas_call(
        place_kernel,
        out_shape=(shape, shape),
        in_specs=[vmem, vmem],
        out_specs=(hbm, hbm),
        scratch_shapes=[dma((2, rows))],
        compiler_params=pltpu.CompilerParams(vmem_limit_bytes=8 << 20),
        name="place",
    )(filt, spread)


def solution(mesh):
    placed = (P("mode", "slab", None), P("slab", None), P("mode", "slab", None))
    return jax.shard_map(
        functools.partial(shards, mesh.shape["slab"], mesh.shape["mode"]),
        mesh=mesh,
        in_specs=placed,
        out_specs=(P("mode", "slab", None), P("mode", "slab", None)),
        check_vma=False,
    )
```
